32 devices in a mesh: row: 16 (over z, y, x), col: 2 (over core).
Axes of the slice: x: 2, y: 2, z: 4, core: 2. Of those that a mesh axis runs over, the one named last changes fastest.
Arguments:
- omega_tiles: float32 [128, 24, 128, 128], P('row', 'col'), may hold values from -0.3 to 0.3
- omega_diag: float32 [16384, 128], P(('row', 'col')), may hold values from -0.25 to 2, as said below
- samples: float32 [16384, 128], P(('row', 'col')), may hold values from -6 to 6
- pattern: int32 [128, 24], P('row', 'col'), may hold values from 0 to 127, as said below
Outputs:
- next_tiles: float32 [128, 24, 128, 128], P('row', 'col')
- next_diag: float32 [16384, 128], P(('row', 'col'))
The draws below stay inside these ranges and needn't reach their ends.
Inputs may be any that keep to these rules, and one draw needn't show every extreme that they name: `pattern`: block j stands at slot s of block row i exactly when block i stands at slot s of block row j, and never in the same group of 8 block rows as i. For the block rows of one index of row and the 12 slots of one index of col, at most 8 listed blocks fall in the block rows of any one other index of row, and exactly 8 for some. A block may stand at more than one slot of a row. `omega_diag`: each row's entry on the diagonal of its block lies in 1 to 2; the others lie within -0.25 to 0.25.
All inputs are finite; a program needn't handle non-finite values.
Results may differ from the reference program's by a relative error of at most 0.00012.
Values sent between devices are 32-bit elements; how exact they have to be, the bound alone decides.
A program may use at most 128 MiB of HBM per device.

```python
import jax
import jax.numpy as jnp
import numpy as np
from jax import lax

BS = 128
K = 24
BR_DEV = 8
NS = 128
ITERS = 2
NB = 128
P_SIZE = 16384
N_ROW = 16
N_COL = 2


def draw_samples(key, part):
    key_one = jax.random.fold_in(jax.random.fold_in(key, 11), 0)
    result = jnp.clip(jax.random.normal(key_one, (P_SIZE, NS), jnp.float32), -6.0, 6.0)
    return result.astype(jnp.float32)


def draw_omega_diag(key, part):
    key_one, key_two = jax.random.split(jax.random.fold_in(key, 3))
    spread = jnp.clip(0.05 * jax.random.normal(key_one, (P_SIZE, BS), jnp.float32), -0.25, 0.25)
    pivots = jax.random.uniform(key_two, (P_SIZE, 1), jnp.float32, 1.0, 2.0)
    column_pos = jnp.arange(BS, dtype=jnp.int32)[None, :]
    row_pos = (jnp.arange(P_SIZE, dtype=jnp.int32) % BS)[:, None]
    return jnp.where(column_pos == row_pos, pivots, spread).astype(jnp.float32)


def draw_pattern(key, part):
    slot_count = K // N_COL
    peer_span = N_ROW // 2 - 2
    unit_idx = np.zeros((N_COL, slot_count, BR_DEV), np.int32)
    signs = np.zeros((N_COL, slot_count, BR_DEV), np.int32)
    kinds = np.zeros((N_COL, slot_count, BR_DEV), np.int32)
    local_rows = np.zeros((N_COL, slot_count, BR_DEV), np.int32)
    col_table = np.zeros((N_COL, slot_count, BR_DEV), np.int32)
    leader_ids = {}
    for slot_index in range(slot_count):
        offset = 1 + slot_index % (BR_DEV - 1)
        for member in range(BR_DEV):
            partner = member ^ offset
            if slot_index == 0 and member < 2:
                continue
            leader = min(member, partner)
            if (slot_index, leader) not in leader_ids:
                leader_ids[slot_index, leader] = len(leader_ids)
    units = max(1, len(leader_ids))
    for col_index in range(N_COL):
        for slot_index in range(slot_count):
            offset = 1 + slot_index % (BR_DEV - 1)
            for member in range(BR_DEV):
                partner = member ^ offset
                col_table[col_index, slot_index, member] = col_index
                if slot_index == 0 and member < 2:
                    kinds[col_index, slot_index, member] = 1 + member
                    local_rows[col_index, slot_index, member] = member
                    signs[col_index, slot_index, member] = 1
                else:
                    unit_idx[col_index, slot_index, member] = leader_ids[slot_index, min(member, partner)]
                    signs[col_index, slot_index, member] = 1 if member < partner else -1
                    local_rows[col_index, slot_index, member] = partner
    key_one, key_two = jax.random.split(jax.random.fold_in(key, 7))
    distances = jax.random.permutation(key_one, peer_span).astype(jnp.int32) + 2
    ordering = jax.random.permutation(key_two, units).astype(jnp.int32)
    position = (ordering[jnp.asarray(unit_idx)] + jnp.asarray(col_table)) % peer_span
    paired = (jnp.asarray(signs) * distances[position])[None]
    device_rows = jnp.arange(N_ROW, dtype=jnp.int32)[:, None, None, None]
    neighbour = jnp.where(device_rows % 2 == 0, 1, -1).astype(jnp.int32)
    kind_grid = jnp.asarray(kinds)[None]
    offsets = jnp.where(kind_grid == 0, paired, jnp.where(kind_grid == 1, N_ROW // 2, neighbour))
    target = (device_rows + offsets + N_ROW) % N_ROW * BR_DEV + jnp.asarray(local_rows)[None]
    return jnp.transpose(target, (0, 3, 1, 2)).reshape(N_ROW * BR_DEV, K).astype(jnp.int32)


def block_scale(key, shape, shards, smallest, largest):
    loudness = 1.0
    for axis_at, blocks in shards:
        steps = jax.random.uniform(jax.random.fold_in(jax.random.fold_in(key, 6), axis_at), (blocks,), jnp.float32, smallest / len(shards), largest / len(shards))
        loudness = loudness * jnp.repeat(jnp.exp(steps), shape[axis_at] // blocks).reshape((-1,) + (1,) * (len(shape) - 1 - axis_at))
    return loudness


def scatter_about(key, extent, deviation, bound, cuts=(), held_as=jnp.bfloat16):
    array = deviation * jax.random.normal(key, extent, jnp.float32)
    if cuts:
        array = array * block_scale(key, extent, cuts, -0.22, 0.18)
    return jnp.clip(array, -bound, bound).astype(held_as)


def setup_inputs(seed: int = 0) -> dict:
    key_list = jax.random.split(jax.random.key(seed), 5)
    omega_tiles = scatter_about(key_list[0], (NB, K, BS, BS), 0.05, 0.3, ((0, 16), (1, 2)), jnp.float32)
    omega_diag = draw_omega_diag(jax.random.fold_in(key_list[4], 71), 0)
    samples = draw_samples(jax.random.fold_in(key_list[4], 71), 0)
    pattern = draw_pattern(jax.random.fold_in(key_list[4], 71), 0)
    return dict(omega_tiles=omega_tiles, omega_diag=omega_diag, samples=samples, pattern=pattern)


step_size = 0.2
shrink_weight = 0.05
ridge_weight = 0.1


def soft_shrink(values, threshold):
    return values - jnp.clip(values, -threshold, threshold)


def reference(omega_tiles, omega_diag, samples, pattern):
    highest = lax.Precision.HIGHEST
    x_blocks = samples.reshape(NB, BS, NS)
    x_tiles = x_blocks[pattern]
    slot_ids = jnp.arange(K, dtype=jnp.int32)[None, :]
    identity = jnp.eye(BS, dtype=jnp.float32)
    tile_vals = omega_tiles
    diag_vals = omega_diag.reshape(NB, BS, BS)
    for sweep_index in range(ITERS):
        products = jnp.einsum("ikm,imn->ikn", diag_vals, x_blocks, precision=highest)
        products = products + jnp.einsum("iskm,ismn->ikn", tile_vals, x_tiles, precision=highest)
        cross_terms = jnp.einsum("ikn,isqn->iskq", products, x_tiles, precision=highest)
        mirror = jnp.swapaxes(cross_terms[pattern, slot_ids], 2, 3)
        gradient = (cross_terms + mirror) * (0.5 / NS) + ridge_weight * tile_vals
        tile_vals = soft_shrink(tile_vals - step_size * gradient, step_size * shrink_weight)
        self_cross = jnp.einsum("ikn,iqn->ikq", products, x_blocks, precision=highest)
        pivots = jnp.diagonal(diag_vals, axis1=1, axis2=2)
        diag_grad = (self_cross + jnp.swapaxes(self_cross, 1, 2)) * (0.5 / NS) + ridge_weight * diag_vals
        diag_grad = diag_grad - identity * (1.0 / pivots)[:, :, None]
        stepped = diag_vals - step_size * diag_grad
        diag_vals = identity * stepped + (1.0 - identity) * soft_shrink(stepped, step_size * shrink_weight)
    return tile_vals, diag_vals.reshape(P_SIZE, BS)
```

```python
import jax
import jax.numpy as jnp
from jax import lax
from jax.experimental import pallas as pl
from jax.experimental.pallas import tpu as pltpu
from jax.sharding import PartitionSpec as P

ITERS = 2


step_size = 0.2
shrink_weight = 0.05
ridge_weight = 0.1


def soft_shrink(values, threshold):
    return values - jnp.clip(values, -threshold, threshold)


def listed_sweeps(omega_tiles, omega_diag, samples, pattern):
    highest = lax.Precision.HIGHEST
    row_count = lax.axis_size("row")
    col_count = lax.axis_size("col")
    my_row = lax.axis_index("row")
    my_col = lax.axis_index("col")
    block_rows = omega_tiles.shape[0]
    slot_count = omega_tiles.shape[1]
    block_size = omega_tiles.shape[2]
    sample_count = samples.shape[1]
    diag_blocks = block_rows // col_count
    all_blocks = block_rows * row_count
    peer_span = row_count // 2 - 2
    capacity = max(1, (slot_count * block_rows // 2 - 1 + peer_span - 1) // peer_span)
    tile_count = block_rows * slot_count
    x_rows = lax.all_gather(samples, "col", axis=0, tiled=True)
    x_blocks = x_rows.reshape(block_rows, block_size, sample_count)
    slot_ids = my_col * slot_count + jnp.arange(slot_count, dtype=jnp.int32)
    own_blocks = my_row * block_rows + jnp.arange(block_rows, dtype=jnp.int32)
    peer_row = (pattern // block_rows).reshape(tile_count)
    order_key = (
        slot_ids[None, :] * all_blocks + jnp.minimum(own_blocks[:, None], pattern)
    ).reshape(tile_count)
    same_peer = peer_row[:, None] == peer_row[None, :]
    before = order_key[None, :] < order_key[:, None]
    peer_rank = jnp.sum((same_peer & before).astype(jnp.int32), axis=1)
    dest_slot = peer_row * capacity + peer_rank
    source_row = jnp.arange(tile_count, dtype=jnp.int32) // slot_count

    def pack_slots(values):
        empty_slots = jnp.zeros((row_count * capacity,) + values.shape[1:], jnp.float32)
        return empty_slots.at[dest_slot].set(values)

    def unpack_slots(received):
        return received[dest_slot].reshape((block_rows, slot_count) + received.shape[1:])

    x_tiles = unpack_slots(
        lax.all_to_all(
            pack_slots(x_blocks[source_row]), "row", split_axis=0, concat_axis=0, tiled=True
        )
    )
    first_diag = my_col * diag_blocks
    x_diag = lax.dynamic_slice_in_dim(x_blocks, first_diag, diag_blocks, 0)
    identity = jnp.eye(block_size, dtype=jnp.float32)
    tile_vals = omega_tiles
    diag_vals = omega_diag.reshape(diag_blocks, block_size, block_size)
    for sweep_index in range(ITERS):
        row_terms = jnp.einsum("askm,asmn->akn", tile_vals, x_tiles, precision=highest)
        diag_terms = jnp.einsum("bkm,bmn->bkn", diag_vals, x_diag, precision=highest)
        own_terms = lax.dynamic_slice_in_dim(row_terms, first_diag, diag_blocks, 0) + diag_terms
        row_terms = lax.dynamic_update_slice_in_dim(row_terms, own_terms, first_diag, 0)
        products = lax.psum(row_terms, "col")
        cross_terms = jnp.einsum("akn,asqn->askq", products, x_tiles, precision=highest)
        returned = lax.all_to_all(
            pack_slots(products[source_row]), "row", split_axis=0, concat_axis=0, tiled=True
        )
        mirror = jnp.einsum("akn,asqn->askq", x_blocks, unpack_slots(returned), precision=highest)
        gradient = (cross_terms + mirror) * (0.5 / sample_count) + ridge_weight * tile_vals
        tile_vals = soft_shrink(tile_vals - step_size * gradient, step_size * shrink_weight)
        y_diag = lax.dynamic_slice_in_dim(products, first_diag, diag_blocks, 0)
        self_cross = jnp.einsum("bkn,bqn->bkq", y_diag, x_diag, precision=highest)
        pivots = jnp.diagonal(diag_vals, axis1=1, axis2=2)
        diag_grad = (self_cross + jnp.swapaxes(self_cross, 1, 2)) * (
            0.5 / sample_count
        ) + ridge_weight * diag_vals
        diag_grad = diag_grad - identity * (1.0 / pivots)[:, :, None]
        stepped = diag_vals - step_size * diag_grad
        diag_vals = identity * stepped + (1.0 - identity) * soft_shrink(
            stepped, step_size * shrink_weight
        )
    return (tile_vals, diag_vals.reshape(omega_diag.shape))


def halves(values):
    high = values.astype(jnp.bfloat16)
    low = (values - high.astype(jnp.float32)).astype(jnp.bfloat16)
    return high, low


def stacked(values):
    return jnp.concatenate(halves(values), axis=0)


def beside(values):
    return jnp.concatenate(halves(values), axis=1)


def fold(full):
    rows, cols = full.shape[0] // 2, full.shape[1] // 2
    return full[:rows, :cols] + (full[:rows, cols:] + full[rows:, :cols])


def times(left, right):
    return jnp.dot(stacked(left), beside(right), preferred_element_type=jnp.float32)


def doubled(values):
    tall = stacked(values)
    return jnp.concatenate([tall, tall], axis=1)


def times_transposed(left_doubled, rights):
    right = jnp.concatenate([beside(r) for r in rights], axis=0)
    full = lax.dot_general(
        left_doubled, right, (((1,), (1,)), ((), ())), preferred_element_type=jnp.float32
    )
    rows, cols = full.shape[0] // 2, rights[0].shape[0]
    full = full[:rows] + full[rows:]
    return [full[:, n * cols : (n + 1) * cols] for n in range(len(rights))]


def product_row(tile_of, x_of, slot_count):
    left = jnp.concatenate([tile_of(s) for s in range(slot_count)], axis=1)
    right = jnp.concatenate([x_of(s) for s in range(slot_count)], axis=0)
    return fold(times(left, right))


def stepped_diag(diag, pair_sum, sample_count):
    size = diag.shape[0]
    on_diagonal = lax.broadcasted_iota(jnp.int32, (size, size), 0) == lax.broadcasted_iota(
        jnp.int32, (size, size), 1
    )
    gradient = pair_sum * (0.5 / sample_count) + ridge_weight * diag
    gradient = gradient - jnp.where(on_diagonal, 1.0 / jnp.where(on_diagonal, diag, 1.0), 0.0)
    stepped = diag - step_size * gradient
    return jnp.where(on_diagonal, stepped, soft_shrink(stepped, step_size * shrink_weight))


MESH = pl.DeviceIdType.MESH
CORNERS = 4
PARTS = 2
SIGNS = (-1, 1)
SLOT_GROUP = 2
WORK_ROWS = 1


class Place:
    def __init__(self):
        self.row = lax.axis_index("row")
        self.col = lax.axis_index("col")
        self.planes = lax.axis_size("row") // CORNERS
        self.z = self.row // CORNERS
        corner = self.row % CORNERS
        y, x = corner // 2, corner % 2
        self.own = y * 2 + x
        self.beside = y * 2 + (1 - x)
        self.across = (1 - y) * 2 + x
        self.opposite = (1 - y) * 2 + (1 - x)

    def at(self, corner):
        return (self.z * CORNERS + corner, self.col)

    def up(self):
        return (self.row + CORNERS, self.col)

    def down(self):
        return (self.row - CORNERS, self.col)

    def partner(self):
        return (self.row, 1 - self.col)

    def in_plane(self, z, origin):
        middle = self.planes // 2
        low = (z < middle) & (origin >= z) & (origin < middle)
        high = (z >= middle) & (origin >= middle) & (origin <= z)
        return low | high


def greet(place):
    barrier = pltpu.get_barrier_semaphore()
    always = (place.at(place.beside), place.at(place.across), place.partner())
    for other in always:
        pl.semaphore_signal(barrier, inc=1, device_id=other, device_id_type=MESH)

    @pl.when(place.z < place.planes - 1)
    def _():
        pl.semaphore_signal(barrier, inc=1, device_id=place.up(), device_id_type=MESH)

    @pl.when(place.z > 0)
    def _():
        pl.semaphore_signal(barrier, inc=1, device_id=place.down(), device_id_type=MESH)

    upper = (place.z < place.planes - 1).astype(jnp.int32)
    lower = (place.z > 0).astype(jnp.int32)
    pl.semaphore_wait(barrier, len(always) + upper + lower)


def gather(place, all_ref, recv, passed, sent, work=()):
    part = all_ref.shape[0] // (place.planes * CORNERS * 2 * PARTS)
    planes, z = place.planes, place.z

    def copy(kind, origin, corner, q, to, col=None):
        source_row = origin * CORNERS + corner
        col = place.col if col is None else col
        first = ((source_row * 2 + col) * PARTS + q) * part
        ref = all_ref.at[pl.ds(first, part)]
        landed = passed if kind == 4 else recv
        return pltpu.make_async_remote_copy(
            src_ref=ref,
            dst_ref=ref,
            send_sem=sent.at[kind, source_row, q],
            recv_sem=landed.at[source_row, q],
            device_id=to,
            device_id_type=MESH,
        )

    def each_origin(distance, act):
        for sign in SIGNS if distance else (0,):
            origin = z + sign * distance

            @pl.when((origin >= 0) & (origin < planes))
            def _(origin=origin, sign=sign):
                act(origin, sign)

    def arrive(origin, corner, q):
        copy(0, origin, corner, q, place.partner()).wait_recv()

    def own_along(distance, do):
        def act(origin, sign):
            for q in range(PARTS):
                if distance and do == "start":
                    arrive(origin, place.own, q)
                if sign <= 0:

                    @pl.when(z < planes - 1)
                    def _():
                        getattr(copy(0, origin, place.own, q, place.up()), do)()

                if sign >= 0:

                    @pl.when(z > 0)
                    def _():
                        getattr(copy(1, origin, place.own, q, place.down()), do)()

                getattr(copy(4, origin, place.own, q, place.partner()), do)()

        each_origin(distance, act)

    def own_plane(distance, do):
        def act(origin, sign):
            for kind, corner, first in ((2, place.beside, 1), (3, place.across, 0)):
                for q in [p for p in range(PARTS) if p % 2 == first] + [
                    p for p in range(PARTS) if p % 2 != first
                ]:
                    getattr(copy(kind, origin, place.own, q, place.at(corner)), do)()

        each_origin(distance, act)

    def near(distance, do, within):
        def act(origin, sign):
            @pl.when(place.in_plane(z, origin) == within)
            def _():
                relay(origin)

        def relay(origin):
            sides = ((0, place.beside, 3, place.across), (1, place.across, 2, place.beside))
            for relayed in (True, False):
                for side, corner, kind, to in sides:
                    for q in range(PARTS):
                        if (side == q % 2) != relayed:
                            continue
                        if do == "start":
                            arrive(origin, corner, q)
                        if relayed and within:
                            getattr(copy(kind, origin, corner, q, place.at(to)), do)()

                        getattr(copy(4, origin, corner, q, place.partner()), do)()

        each_origin(distance, act)

    def far(distance, do, within):
        def act(origin, sign):
            @pl.when(place.in_plane(z, origin) == within)
            def _():
                for q in range(PARTS):
                    if do == "start":
                        arrive(origin, place.opposite, q)
                    if sign <= 0:

                        @pl.when((z < planes - 1) & jnp.logical_not(place.in_plane(z + 1, origin)))
                        def _():
                            getattr(copy(0, origin, place.opposite, q, place.up()), do)()

                    if sign >= 0:

                        @pl.when((z > 0) & jnp.logical_not(place.in_plane(z - 1, origin)))
                        def _():
                            getattr(copy(1, origin, place.opposite, q, place.down()), do)()

                    getattr(copy(4, origin, place.opposite, q, place.partner()), do)()

        each_origin(distance, act)

    steps = [(own_along, 0), (own_plane, 0)]
    for distance in range(planes):
        if distance + 1 < planes:
            steps += [(own_along, distance + 1)]
        if distance == 0:
            steps += [(near, 0, True), (own_plane, 1), (far, 0, True)]
        else:
            if distance + 1 < planes:
                steps += [(own_plane, distance + 1)]
                steps += [(far, distance, False), (near, distance, True)]
    for distance in range(1, planes):
        steps += [(near, distance, False), (far, distance, True)]
        if distance + 1 == planes:
            steps += [(near, distance, True), (far, distance, False)]

    def passed_on(origin, corner):
        for q in range(PARTS):
            copy(4, origin, corner, q, place.partner(), 1 - place.col).wait_recv()

    def run(do):
        pending = list(work)
        for count, step in enumerate(steps):
            step[0](step[1], do, *step[2:])
            if do == "start" and count == 2:
                passed_on(z, place.own)
            if do == "start" and count >= 2 and pending:
                pending.pop(0)()
        if do == "start":
            for unit in pending:
                unit()

    run("start")
    run("wait_send")

    @pl.loop(0, planes)
    def _(origin):
        for corner in range(CORNERS):

            @pl.when((origin != z) | (corner != place.own))
            def _():
                passed_on(origin, corner)


def slot_groups(slot_count):
    return [range(s, min(s + SLOT_GROUP, slot_count)) for s in range(0, slot_count, SLOT_GROUP)]


def mirror_row(a, first_own, pattern, tiles, x_all, y_all, stepped, sample_count):
    slot_count = tiles.shape[1]
    pair_weight = step_size * 0.5 / sample_count
    left = doubled(x_all[first_own + a])
    for group in slot_groups(slot_count):
        found = times_transposed(left, [y_all[pattern[a, s]] for s in group])
        for s, mirror in zip(group, found):
            stepped[a, s] = soft_shrink(
                tiles[a, s] - pair_weight * mirror, step_size * shrink_weight
            )


def sweeps_kernel(
    pattern,
    tiles_in,
    diag_in,
    samples,
    tiles,
    x_all,
    y_last,
    diag,
    y_part,
    y_in,
    recv,
    passed,
    sent,
    local,
    pair,
    *y_before,
):
    place = Place()
    y_every = [*y_before, y_last]
    block_rows, slot_count = tiles.shape[:2]
    diag_blocks = diag_in.shape[0]
    sample_count = x_all.shape[2]
    first_own = place.row * block_rows
    first_diag = place.col * diag_blocks
    first_other = (1 - place.col) * diag_blocks
    load = pltpu.make_async_copy(tiles_in, tiles, local.at[0])
    load_diag = pltpu.make_async_copy(diag_in, diag, local.at[2])
    mine = pl.ds(first_own + first_diag, diag_blocks)
    take = pltpu.make_async_copy(samples, x_all.at[mine], local.at[1])
    take.start()
    load.start()
    load_diag.start()
    greet(place)
    take.wait()
    gather(place, x_all, recv.at[0], passed.at[0], sent)
    load.wait()
    load_diag.wait()

    def y_row(a):
        y_part[a] = product_row(lambda s: tiles[a, s], lambda s: x_all[pattern[a, s]], slot_count)

    def send_partial(sweep):
        return pltpu.make_async_remote_copy(
            src_ref=y_part.at[pl.ds(first_other, diag_blocks)],
            dst_ref=y_in.at[sweep],
            send_sem=pair.at[0, sweep],
            recv_sem=pair.at[1, sweep],
            device_id=place.partner(),
            device_id_type=MESH,
        )

    groups = slot_groups(slot_count)
    pair_weight = step_size * 0.5 / sample_count

    def cross_tiles(a, y_all):
        left = doubled(y_all[first_own + a])
        for group in groups:
            found = times_transposed(left, [x_all[pattern[a, s]] for s in group])
            for s, cross in zip(group, found):
                tiles[a, s] = (1.0 - step_size * ridge_weight) * tiles[a, s] - pair_weight * cross

    def mirror_tiles(a, y_all):
        mirror_row(a, first_own, pattern, tiles, x_all, y_all, tiles, sample_count)

    def step_own(d, y_all):
        own = first_own + first_diag + d
        pair_sum = (
            times_transposed(doubled(y_all[own]), [x_all[own]])[0]
            + times_transposed(doubled(x_all[own]), [y_all[own]])[0]
        )
        diag[d] = stepped_diag(diag[d], pair_sum, sample_count)

    def products(sweep, y_all, before):
        @pl.loop(0, diag_blocks)
        def _(d):
            before(first_other + d)
            y_row(first_other + d)

        sending = send_partial(sweep)
        sending.start()

        @pl.loop(0, diag_blocks)
        def _(d):
            before(first_diag + d)
            y_row(first_diag + d)
            y_part[first_diag + d] += fold(times(diag[d], x_all[first_own + first_diag + d]))

        sending.wait()

        @pl.loop(0, diag_blocks)
        def _(d):
            y_all[first_own + first_diag + d] = y_part[first_diag + d] + y_in[sweep, d]

        def unit(first):
            @pl.loop(0, WORK_ROWS)
            def _(n):
                cross_tiles((first_diag + first + n) % block_rows, y_all)

        def unit_diag():
            @pl.loop(0, diag_blocks)
            def _(d):
                step_own(d, y_all)

        work = [lambda first=first: unit(first) for first in range(0, block_rows, WORK_ROWS)]
        work.insert(1, unit_diag)
        gather(place, y_all, recv.at[1 + sweep], passed.at[1 + sweep], sent, work)

    products(0, y_every[0], lambda a: None)
    for sweep in range(ITERS - 1):
        products(
            sweep + 1, y_every[sweep + 1], lambda a: mirror_tiles(a, y_every[sweep])
        )


def finish_kernel(pattern, tiles, x_all, y_all, diag_in, tiles_out, diag_out, ready, sems):
    block_rows, slot_count = tiles.shape[:2]
    sample_count = x_all.shape[2]
    first_own = lax.axis_index("row") * block_rows
    diag_out[...] = diag_in[...]

    def store(a):
        return pltpu.make_async_copy(ready.at[a], tiles_out.at[a], sems.at[a])

    @pl.loop(0, block_rows)
    def _(a):
        mirror_row(a, first_own, pattern, tiles, x_all, y_all, ready, sample_count)
        store(a).start()

    @pl.loop(0, block_rows)
    def _(a):
        store(a).wait()


def gathered_sweeps(omega_tiles, omega_diag, samples, pattern):
    block_rows, slot_count, size, _ = omega_tiles.shape
    row_count = lax.axis_size("row")
    sample_count = samples.shape[1]
    diag_blocks = block_rows // lax.axis_size("col")
    diag = omega_diag.reshape(diag_blocks, size, size)
    every = (row_count * block_rows, size, sample_count)
    in_vmem = pl.BlockSpec(memory_space=pltpu.VMEM)
    in_hbm = pl.BlockSpec(memory_space=pltpu.HBM)
    in_smem = pl.BlockSpec(memory_space=pltpu.SMEM)
    tiles, x_all, y_all, diag = pl.pallas_call(
        sweeps_kernel,
        name="sweeps",
        out_shape=[
            pltpu.VMEM(omega_tiles.shape, jnp.float32),
            pltpu.VMEM(every, jnp.float32),
            pltpu.VMEM(every, jnp.float32),
            pltpu.VMEM(diag.shape, jnp.float32),
        ],
        in_specs=[in_smem, in_hbm, in_hbm, in_hbm],
        out_specs=[in_vmem] * 4,
        scratch_shapes=[
            pltpu.VMEM((block_rows, size, sample_count), jnp.float32),
            pltpu.VMEM((ITERS, diag_blocks, size, sample_count), jnp.float32),
            pltpu.SemaphoreType.DMA((1 + ITERS, row_count, PARTS)),
            pltpu.SemaphoreType.DMA((1 + ITERS, row_count, PARTS)),
            pltpu.SemaphoreType.DMA((5, row_count, PARTS)),
            pltpu.SemaphoreType.DMA((3,)),
            pltpu.SemaphoreType.DMA((2, ITERS)),
        ]
        + [pltpu.VMEM(every, jnp.float32)] * (ITERS - 1),
        compiler_params=pltpu.CompilerParams(
            collective_id=0, has_side_effects=True, vmem_limit_bytes=40 * 2**20
        ),
    )(
        pattern,
        *(
            pltpu.with_memory_space_constraint(v, pltpu.HBM)
            for v in (omega_tiles, diag, samples.reshape(diag_blocks, size, sample_count))
        ),
    )
    held = [pltpu.with_memory_space_constraint(v, pltpu.VMEM) for v in (tiles, x_all, y_all, diag)]
    tiles, diag = pl.pallas_call(
        finish_kernel,
        name="finish",
        out_shape=[
            jax.ShapeDtypeStruct(omega_tiles.shape, jnp.float32),
            jax.ShapeDtypeStruct(diag.shape, jnp.float32),
        ],
        in_specs=[in_smem] + [in_vmem] * 4,
        out_specs=[in_hbm, in_vmem],
        scratch_shapes=[
            pltpu.VMEM(omega_tiles.shape, jnp.float32),
            pltpu.SemaphoreType.DMA((block_rows,)),
        ],
        compiler_params=pltpu.CompilerParams(vmem_limit_bytes=16 * 2**20),
    )(pattern, *held)
    return tiles, diag.reshape(omega_diag.shape)


def on_device(omega_tiles, omega_diag, samples, pattern):
    row_count = lax.axis_size("row")
    block_rows, slot_count = omega_tiles.shape[:2]
    peer_span = row_count // 2 - 2
    capacity = max(1, (slot_count * block_rows // 2 - 1 + peer_span - 1) // peer_span)
    whole_gather = 2 * capacity >= block_rows and lax.axis_size("col") == 2 and row_count % 4 == 0
    sweeps = gathered_sweeps if whole_gather else listed_sweeps
    return sweeps(omega_tiles, omega_diag, samples, pattern)


def solution(mesh):
    in_specs = (
        P("row", "col", None, None),
        P(("row", "col"), None),
        P(("row", "col"), None),
        P("row", "col"),
    )
    out_specs = (P("row", "col", None, None), P(("row", "col"), None))
    return jax.shard_map(
        on_device, mesh=mesh, in_specs=in_specs, out_specs=out_specs, check_vma=False
    )
```

```python
import jax
import jax.numpy as jnp
from jax import lax
from jax.experimental import pallas as pl
from jax.experimental.pallas import tpu as pltpu
from jax.sharding import PartitionSpec as P

ITERS = 2


step_size = 0.2
shrink_weight = 0.05
ridge_weight = 0.1


def soft_shrink(values, threshold):
    return values - jnp.clip(values, -threshold, threshold)


def listed_sweeps(omega_tiles, omega_diag, samples, pattern):
    highest = lax.Precision.HIGHEST
    row_count = lax.axis_size("row")
    col_count = lax.axis_size("col")
    my_row = lax.axis_index("row")
    my_col = lax.axis_index("col")
    block_rows = omega_tiles.shape[0]
    slot_count = omega_tiles.shape[1]
    block_size = omega_tiles.shape[2]
    sample_count = samples.shape[1]
    diag_blocks = block_rows // col_count
    all_blocks = block_rows * row_count
    peer_span = row_count // 2 - 2
    capacity = max(1, (slot_count * block_rows // 2 - 1 + peer_span - 1) // peer_span)
    tile_count = block_rows * slot_count
    x_rows = lax.all_gather(samples, "col", axis=0, tiled=True)
    x_blocks = x_rows.reshape(block_rows, block_size, sample_count)
    slot_ids = my_col * slot_count + jnp.arange(slot_count, dtype=jnp.int32)
    own_blocks = my_row * block_rows + jnp.arange(block_rows, dtype=jnp.int32)
    peer_row = (pattern // block_rows).reshape(tile_count)
    order_key = (
        slot_ids[None, :] * all_blocks + jnp.minimum(own_blocks[:, None], pattern)
    ).reshape(tile_count)
    same_peer = peer_row[:, None] == peer_row[None, :]
    before = order_key[None, :] < order_key[:, None]
    peer_rank = jnp.sum((same_peer & before).astype(jnp.int32), axis=1)
    dest_slot = peer_row * capacity + peer_rank
    source_row = jnp.arange(tile_count, dtype=jnp.int32) // slot_count

    def pack_slots(values):
        empty_slots = jnp.zeros((row_count * capacity,) + values.shape[1:], jnp.float32)
        return empty_slots.at[dest_slot].set(values)

    def unpack_slots(received):
        return received[dest_slot].reshape((block_rows, slot_count) + received.shape[1:])

    x_tiles = unpack_slots(
        lax.all_to_all(
            pack_slots(x_blocks[source_row]), "row", split_axis=0, concat_axis=0, tiled=True
        )
    )
    first_diag = my_col * diag_blocks
    x_diag = lax.dynamic_slice_in_dim(x_blocks, first_diag, diag_blocks, 0)
    identity = jnp.eye(block_size, dtype=jnp.float32)
    tile_vals = omega_tiles
    diag_vals = omega_diag.reshape(diag_blocks, block_size, block_size)
    for sweep_index in range(ITERS):
        row_terms = jnp.einsum("askm,asmn->akn", tile_vals, x_tiles, precision=highest)
        diag_terms = jnp.einsum("bkm,bmn->bkn", diag_vals, x_diag, precision=highest)
        own_terms = lax.dynamic_slice_in_dim(row_terms, first_diag, diag_blocks, 0) + diag_terms
        row_terms = lax.dynamic_update_slice_in_dim(row_terms, own_terms, first_diag, 0)
        products = lax.psum(row_terms, "col")
        cross_terms = jnp.einsum("akn,asqn->askq", products, x_tiles, precision=highest)
        returned = lax.all_to_all(
            pack_slots(products[source_row]), "row", split_axis=0, concat_axis=0, tiled=True
        )
        mirror = jnp.einsum("akn,asqn->askq", x_blocks, unpack_slots(returned), precision=highest)
        gradient = (cross_terms + mirror) * (0.5 / sample_count) + ridge_weight * tile_vals
        tile_vals = soft_shrink(tile_vals - step_size * gradient, step_size * shrink_weight)
        y_diag = lax.dynamic_slice_in_dim(products, first_diag, diag_blocks, 0)
        self_cross = jnp.einsum("bkn,bqn->bkq", y_diag, x_diag, precision=highest)
        pivots = jnp.diagonal(diag_vals, axis1=1, axis2=2)
        diag_grad = (self_cross + jnp.swapaxes(self_cross, 1, 2)) * (
            0.5 / sample_count
        ) + ridge_weight * diag_vals
        diag_grad = diag_grad - identity * (1.0 / pivots)[:, :, None]
        stepped = diag_vals - step_size * diag_grad
        diag_vals = identity * stepped + (1.0 - identity) * soft_shrink(
            stepped, step_size * shrink_weight
        )
    return (tile_vals, diag_vals.reshape(omega_diag.shape))


def halves(values):
    high = values.astype(jnp.bfloat16)
    low = (values - high.astype(jnp.float32)).astype(jnp.bfloat16)
    return high, low


def stacked(values):
    return jnp.concatenate(halves(values), axis=0)


def beside(values):
    return jnp.concatenate(halves(values), axis=1)


def fold(full):
    rows, cols = full.shape[0] // 2, full.shape[1] // 2
    return full[:rows, :cols] + (full[:rows, cols:] + full[rows:, :cols])


def times(left, right):
    return jnp.dot(stacked(left), beside(right), preferred_element_type=jnp.float32)


def doubled(values):
    tall = stacked(values)
    return jnp.concatenate([tall, tall], axis=1)


def times_transposed(left_doubled, rights):
    right = jnp.concatenate([beside(r) for r in rights], axis=0)
    full = lax.dot_general(
        left_doubled, right, (((1,), (1,)), ((), ())), preferred_element_type=jnp.float32
    )
    rows, cols = full.shape[0] // 2, rights[0].shape[0]
    full = full[:rows] + full[rows:]
    return [full[:, n * cols : (n + 1) * cols] for n in range(len(rights))]


def product_row(tile_of, x_of, slot_count):
    left = jnp.concatenate([tile_of(s) for s in range(slot_count)], axis=1)
    right = jnp.concatenate([x_of(s) for s in range(slot_count)], axis=0)
    return fold(times(left, right))


def stepped_diag(diag, pair_sum, sample_count):
    size = diag.shape[0]
    on_diagonal = lax.broadcasted_iota(jnp.int32, (size, size), 0) == lax.broadcasted_iota(
        jnp.int32, (size, size), 1
    )
    gradient = pair_sum * (0.5 / sample_count) + ridge_weight * diag
    gradient = gradient - jnp.where(on_diagonal, 1.0 / jnp.where(on_diagonal, diag, 1.0), 0.0)
    stepped = diag - step_size * gradient
    return jnp.where(on_diagonal, stepped, soft_shrink(stepped, step_size * shrink_weight))


MESH = pl.DeviceIdType.MESH
CORNERS = 4
SLOT_GROUP = 2
SEND_US = 1.44
HOP_US = 1.7
LEAD_US = 1.5
ROW_US = (0.55, 1.1)
UNIT_US = 1.44
INNER, OUTER, ACROSS_X, ACROSS_Y, PARTNER = range(5)


class Place:
    def __init__(self):
        self.row = lax.axis_index("row")
        self.col = lax.axis_index("col")
        self.planes = lax.axis_size("row") // CORNERS
        z = self.row // CORNERS
        corner = self.row % CORNERS
        y, x = corner // 2, corner % 2
        upper = (z >= self.planes // 2).astype(jnp.int32)
        self.sign = 1 - 2 * upper
        self.base = upper * (self.planes - 1)
        self.plane = self.base + self.sign * z
        self.corners = {
            "own": corner,
            "beside": y * 2 + (1 - x),
            "across": (1 - y) * 2 + x,
            "opposite": (1 - y) * 2 + (1 - x),
        }
        first = z * CORNERS
        self.target = {
            INNER: (self.row + CORNERS * self.sign, self.col),
            OUTER: (self.row - CORNERS * self.sign, self.col),
            ACROSS_X: (first + self.corners["beside"], self.col),
            ACROSS_Y: (first + self.corners["across"], self.col),
            PARTNER: (self.row, 1 - self.col),
        }

    def source(self, origin, corner):
        return (self.base + self.sign * origin) * CORNERS + self.corners[corner]


def in_plane(planes, plane, origin):
    middle = planes // 2
    if plane < middle:
        return plane <= origin < middle
    return middle <= origin <= plane


def onward(planes, plane, origin, corner, part):
    found = []
    rising = origin <= plane < planes - 1
    falling = origin >= plane > 0
    if corner == "own":
        if rising:
            found.append((INNER, plane + 1, "own"))
        if falling:
            found.append((OUTER, plane - 1, "own"))
        found += [(ACROSS_X, plane, "beside"), (ACROSS_Y, plane, "across")]
    elif corner == "beside":
        if in_plane(planes, plane, origin) and part % 2 == 1:
            found.append((ACROSS_Y, plane, "opposite"))
    elif corner == "across":
        if in_plane(planes, plane, origin) and part % 2 == 0:
            found.append((ACROSS_X, plane, "opposite"))
    else:
        if rising and not in_plane(planes, plane + 1, origin):
            found.append((INNER, plane + 1, "opposite"))
        if falling and not in_plane(planes, plane - 1, origin):
            found.append((OUTER, plane - 1, "opposite"))
    return found


def plan(planes, ready):
    parts = len(ready)
    waiting = {}
    free_at = {}
    acts = [[] for _ in range(planes)]
    events = []
    count = 0
    for plane in range(planes):
        for q in range(parts):
            events.append((ready[q], count, plane, (plane, "own", q), None))
            count += 1
    while events:
        event = min(events)
        events.remove(event)
        now, _, plane, part, link = event
        touched = []
        if link is None:
            origin, corner, q = part
            if (origin, corner) != (plane, "own"):
                acts[plane].append((now, "take", part))
            for out, _, _ in onward(planes, plane, origin, corner, q):
                waiting.setdefault((plane, out), []).append(
                    (abs(plane - origin), now, count, part)
                )
                count += 1
                touched.append((plane, out))
        else:
            touched.append((plane, link))
        for key in touched:
            queue = waiting.get(key, [])
            if not queue or free_at.get(key, -1.0) > now:
                continue
            item = min(queue)
            queue.remove(item)
            free_at[key] = now + SEND_US
            events.append((now + SEND_US, count, plane, None, key[1]))
            count += 1
            sent = item[3]
            if sent[:2] != (plane, "own"):
                acts[plane].append((max(item[1], now - LEAD_US) + 1e-6, "send", key[1], sent))
            for out, to, corner in onward(planes, plane, *sent):
                if out == key[1]:
                    events.append(
                        (now + SEND_US + HOP_US, count, to, (sent[0], corner, sent[2]), None)
                    )
                    count += 1
    return [sorted(found, key=lambda act: act[0]) for found in acts]


class Gather:
    def __init__(self, place, all_ref, parts, recv, passed, met, sent, ready):
        self.place, self.all_ref, self.parts = place, all_ref, parts
        self.recv, self.passed, self.met, self.sent = recv, passed, met, sent
        self.size = all_ref.shape[0] // (place.planes * CORNERS * 2 * parts)
        self.near = range((place.planes + 1) // 2)
        self.acts = plan(place.planes, ready)

    def copy(self, link, part, col=None):
        origin, corner, q = part
        row = self.place.source(origin, corner)
        col = self.place.col if col is None else col
        ref = self.all_ref.at[pl.ds(((row * 2 + col) * self.parts + q) * self.size, self.size)]
        landed = self.recv.at[row, q] if link != PARTNER else self.passed
        return self.describe(ref, link, landed)

    def describe(self, ref, link, landed):
        return pltpu.make_async_remote_copy(
            src_ref=ref,
            dst_ref=ref,
            send_sem=self.sent.at[link],
            recv_sem=landed,
            device_id=self.place.target[link],
            device_id_type=MESH,
        )

    def own(self, q, col=None):
        col = self.place.col if col is None else col
        first = ((self.place.row * 2 + col) * self.parts + q) * self.size
        return self.all_ref.at[pl.ds(first, self.size)]

    def start_own(self, q):
        ref = self.own(q)
        for link in (ACROSS_X, ACROSS_Y, INNER):
            self.describe(ref, link, self.recv.at[self.place.row, q]).start()

        @pl.when(self.place.plane > 0)
        def _():
            self.describe(ref, OUTER, self.recv.at[self.place.row, q]).start()

        self.describe(ref, PARTNER, self.met.at[q]).start()

    def meet(self, q):
        self.describe(self.own(q, 1 - self.place.col), PARTNER, self.met.at[q]).wait_recv()

    def run(self, after, until):
        for plane in self.near:
            chosen = [act for act in self.acts[plane] if after < act[0] <= until]
            if chosen:

                @pl.when(self.place.plane == plane)
                def _(chosen=chosen):
                    for act in chosen:
                        if act[1] == "take":
                            self.copy(INNER, act[2]).wait_recv()
                            self.copy(PARTNER, act[2]).start()
                        else:
                            self.copy(act[2], act[3]).start()

    def all_passed(self):
        count = (self.place.planes * CORNERS - 1) * self.parts * self.size
        self.describe(self.all_ref.at[pl.ds(0, count)], PARTNER, self.passed).wait_recv()

    def all_sent(self):
        for plane in self.near:

            @pl.when(self.place.plane == plane)
            def _(plane=plane):
                counts = [0] * 5
                for act in self.acts[plane]:
                    counts[PARTNER if act[1] == "take" else act[2]] += 1
                for link in range(5):
                    own = self.parts if link != OUTER or plane > 0 else 0
                    total = (counts[link] + own) * self.size
                    if total:
                        ref = self.all_ref.at[pl.ds(0, total)]
                        self.describe(ref, link, self.passed).wait_send()


def greet(place):
    barrier = pltpu.get_barrier_semaphore()
    for link in (ACROSS_X, ACROSS_Y, PARTNER, INNER):
        pl.semaphore_signal(barrier, inc=1, device_id=place.target[link], device_id_type=MESH)

    @pl.when(place.plane > 0)
    def _():
        pl.semaphore_signal(barrier, inc=1, device_id=place.target[OUTER], device_id_type=MESH)

    pl.semaphore_wait(barrier, 4 + (place.plane > 0).astype(jnp.int32))


def slot_groups(slot_count):
    return [range(s, min(s + SLOT_GROUP, slot_count)) for s in range(0, slot_count, SLOT_GROUP)]


def mirror_row(a, first_own, pattern, tiles, x_all, y_all, stepped, sample_count):
    slot_count = tiles.shape[1]
    pair_weight = step_size * 0.5 / sample_count
    left = doubled(x_all[first_own + a])
    for group in slot_groups(slot_count):
        found = times_transposed(left, [y_all[pattern[a, s]] for s in group])
        for s, mirror in zip(group, found):
            stepped[a, s] = soft_shrink(
                tiles[a, s] - pair_weight * mirror, step_size * shrink_weight
            )


def sweeps_kernel(
    pattern,
    tiles_in,
    diag_in,
    samples,
    tiles,
    x_all,
    y_last,
    diag,
    y_part,
    y_in,
    recv,
    passed,
    met,
    sent,
    local,
    pair,
    *y_before,
):
    place = Place()
    y_every = [*y_before, y_last]
    block_rows, slot_count = tiles.shape[:2]
    diag_blocks = diag_in.shape[0]
    sample_count = x_all.shape[2]
    first_own = place.row * block_rows
    first_diag = place.col * diag_blocks
    first_other = (1 - place.col) * diag_blocks
    load = pltpu.make_async_copy(tiles_in, tiles, local.at[0])
    load_diag = pltpu.make_async_copy(diag_in, diag, local.at[2])
    mine = pl.ds(first_own + first_diag, diag_blocks)
    take = pltpu.make_async_copy(samples, x_all.at[mine], local.at[1])
    take.start()
    load.start()
    load_diag.start()

    def gather(n, all_ref, ready):
        return Gather(
            place, all_ref, diag_blocks, recv.at[n], passed.at[n], met.at[n], sent.at[n], ready
        )

    forever = float("inf")
    gathers = [gather(0, x_all, [0.0] * diag_blocks)]
    greet(place)
    take.wait()
    for q in range(diag_blocks):
        gathers[0].start_own(q)
    gathers[0].run(-1.0, forever)
    for q in range(diag_blocks):
        gathers[0].meet(q)
    gathers[0].all_passed()
    load.wait()
    load_diag.wait()

    def y_row(a):
        y_part[a] = product_row(lambda s: tiles[a, s], lambda s: x_all[pattern[a, s]], slot_count)

    def send_partial(sweep, d):
        return pltpu.make_async_remote_copy(
            src_ref=y_part.at[first_other + d],
            dst_ref=y_in.at[sweep, d],
            send_sem=pair.at[0, sweep, d],
            recv_sem=pair.at[1, sweep, d],
            device_id=place.target[PARTNER],
            device_id_type=MESH,
        )

    groups = slot_groups(slot_count)
    pair_weight = step_size * 0.5 / sample_count

    def cross_tiles(a, y_all):
        left = doubled(y_all[first_own + a])
        for group in groups:
            found = times_transposed(left, [x_all[pattern[a, s]] for s in group])
            for s, cross in zip(group, found):
                tiles[a, s] = (1.0 - step_size * ridge_weight) * tiles[a, s] - pair_weight * cross

    def mirror_tiles(a, y_all):
        mirror_row(a, first_own, pattern, tiles, x_all, y_all, tiles, sample_count)

    def step_own(d, y_all):
        own = first_own + first_diag + d
        pair_sum = (
            times_transposed(doubled(y_all[own]), [x_all[own]])[0]
            + times_transposed(doubled(x_all[own]), [y_all[own]])[0]
        )
        diag[d] = stepped_diag(diag[d], pair_sum, sample_count)

    def products(sweep, before):
        y_all = y_every[sweep]
        row_us = ROW_US[min(sweep, 1)]
        ready = [2 * row_us * d for d in range(diag_blocks)]
        going = gather(1 + sweep, y_all, ready)
        gathers.append(going)

        def finalize(d):
            send_partial(sweep, d).wait()
            y_all[first_own + first_diag + d] = y_part[first_diag + d] + y_in[sweep, d]
            going.start_own(d)

        @pl.loop(0, diag_blocks)
        def _(d):
            before(first_other + d)
            y_row(first_other + d)
            send_partial(sweep, d).start()

            @pl.when(d > 0)
            def _():
                finalize(d - 1)

            for k in range(1, diag_blocks):

                @pl.when(d == k)
                def _(k=k):
                    going.run(ready[k - 1] - 2 * row_us, ready[k - 1])

            before(first_diag + d)
            y_row(first_diag + d)
            y_part[first_diag + d] += fold(times(diag[d], x_all[first_own + first_diag + d]))

        finalize(diag_blocks - 1)

        @pl.loop(0, block_rows)
        def _(n):
            for k in range(block_rows):

                @pl.when(n == k)
                def _(k=k):
                    if k == diag_blocks:
                        for q in range(diag_blocks):
                            going.meet(q)
                    begin = ready[-1] + k * UNIT_US
                    going.run(ready[-2] if k == 0 else begin - UNIT_US, begin)

            cross_tiles((first_diag + n) % block_rows, y_all)

            @pl.when(n < diag_blocks)
            def _():
                step_own(n, y_all)

        going.run(ready[-1] + (block_rows - 1) * UNIT_US, forever)
        going.all_passed()

    products(0, lambda a: None)
    for sweep in range(1, ITERS):
        products(sweep, lambda a: mirror_tiles(a, y_every[sweep - 1]))
    for done in gathers:
        done.all_sent()


def finish_kernel(pattern, tiles, x_all, y_all, diag_in, tiles_out, diag_out, ready, sems):
    block_rows, slot_count = tiles.shape[:2]
    sample_count = x_all.shape[2]
    first_own = lax.axis_index("row") * block_rows
    diag_out[...] = diag_in[...]

    def store(a):
        return pltpu.make_async_copy(ready.at[a], tiles_out.at[a], sems.at[a])

    @pl.loop(0, block_rows)
    def _(a):
        mirror_row(a, first_own, pattern, tiles, x_all, y_all, ready, sample_count)
        store(a).start()

    @pl.loop(0, block_rows)
    def _(a):
        store(a).wait()


def gathered_sweeps(omega_tiles, omega_diag, samples, pattern):
    block_rows, slot_count, size, _ = omega_tiles.shape
    row_count = lax.axis_size("row")
    sample_count = samples.shape[1]
    diag_blocks = block_rows // lax.axis_size("col")
    diag = omega_diag.reshape(diag_blocks, size, size)
    every = (row_count * block_rows, size, sample_count)
    in_vmem = pl.BlockSpec(memory_space=pltpu.VMEM)
    in_hbm = pl.BlockSpec(memory_space=pltpu.HBM)
    in_smem = pl.BlockSpec(memory_space=pltpu.SMEM)
    tiles, x_all, y_all, diag = pl.pallas_call(
        sweeps_kernel,
        name="sweeps",
        out_shape=[
            pltpu.VMEM(omega_tiles.shape, jnp.float32),
            pltpu.VMEM(every, jnp.float32),
            pltpu.VMEM(every, jnp.float32),
            pltpu.VMEM(diag.shape, jnp.float32),
        ],
        in_specs=[in_smem, in_hbm, in_hbm, in_hbm],
        out_specs=[in_vmem] * 4,
        scratch_shapes=[
            pltpu.VMEM((block_rows, size, sample_count), jnp.float32),
            pltpu.VMEM((ITERS, diag_blocks, size, sample_count), jnp.float32),
            pltpu.SemaphoreType.DMA((1 + ITERS, row_count, diag_blocks)),
            pltpu.SemaphoreType.DMA((1 + ITERS,)),
            pltpu.SemaphoreType.DMA((1 + ITERS, diag_blocks)),
            pltpu.SemaphoreType.DMA((1 + ITERS, 5)),
            pltpu.SemaphoreType.DMA((3,)),
            pltpu.SemaphoreType.DMA((2, ITERS, diag_blocks)),
        ]
        + [pltpu.VMEM(every, jnp.float32)] * (ITERS - 1),
        compiler_params=pltpu.CompilerParams(
            collective_id=0, has_side_effects=True, vmem_limit_bytes=40 * 2**20
        ),
    )(
        pattern,
        *(
            pltpu.with_memory_space_constraint(v, pltpu.HBM)
            for v in (omega_tiles, diag, samples.reshape(diag_blocks, size, sample_count))
        ),
    )
    held = [pltpu.with_memory_space_constraint(v, pltpu.VMEM) for v in (tiles, x_all, y_all, diag)]
    tiles, diag = pl.pallas_call(
        finish_kernel,
        name="finish",
        out_shape=[
            jax.ShapeDtypeStruct(omega_tiles.shape, jnp.float32),
            jax.ShapeDtypeStruct(diag.shape, jnp.float32),
        ],
        in_specs=[in_smem] + [in_vmem] * 4,
        out_specs=[in_hbm, in_vmem],
        scratch_shapes=[
            pltpu.VMEM(omega_tiles.shape, jnp.float32),
            pltpu.SemaphoreType.DMA((block_rows,)),
        ],
        compiler_params=pltpu.CompilerParams(vmem_limit_bytes=16 * 2**20),
    )(pattern, *held)
    return tiles, diag.reshape(omega_diag.shape)


def on_device(omega_tiles, omega_diag, samples, pattern):
    row_count = lax.axis_size("row")
    block_rows, slot_count = omega_tiles.shape[:2]
    peer_span = row_count // 2 - 2
    capacity = max(1, (slot_count * block_rows // 2 - 1 + peer_span - 1) // peer_span)
    whole_gather = 2 * capacity >= block_rows and lax.axis_size("col") == 2 and row_count % 8 == 0
    sweeps = gathered_sweeps if whole_gather else listed_sweeps
    return sweeps(omega_tiles, omega_diag, samples, pattern)


def solution(mesh):
    in_specs = (
        P("row", "col", None, None),
        P(("row", "col"), None),
        P(("row", "col"), None),
        P("row", "col"),
    )
    out_specs = (P("row", "col", None, None), P(("row", "col"), None))
    return jax.shard_map(
        on_device, mesh=mesh, in_specs=in_specs, out_specs=out_specs, check_vma=False
    )
```

```python
import jax
import jax.numpy as jnp
from jax import lax
from jax.experimental import pallas as pl
from jax.experimental.pallas import tpu as pltpu
from jax.sharding import PartitionSpec as P

ITERS = 2


step_size = 0.2
shrink_weight = 0.05
ridge_weight = 0.1


def soft_shrink(values, threshold):
    return values - jnp.clip(values, -threshold, threshold)


def listed_sweeps(omega_tiles, omega_diag, samples, pattern):
    highest = lax.Precision.HIGHEST
    row_count = lax.axis_size("row")
    col_count = lax.axis_size("col")
    my_row = lax.axis_index("row")
    my_col = lax.axis_index("col")
    block_rows = omega_tiles.shape[0]
    slot_count = omega_tiles.shape[1]
    block_size = omega_tiles.shape[2]
    sample_count = samples.shape[1]
    diag_blocks = block_rows // col_count
    all_blocks = block_rows * row_count
    peer_span = row_count // 2 - 2
    capacity = max(1, (slot_count * block_rows // 2 - 1 + peer_span - 1) // peer_span)
    tile_count = block_rows * slot_count
    x_rows = lax.all_gather(samples, "col", axis=0, tiled=True)
    x_blocks = x_rows.reshape(block_rows, block_size, sample_count)
    slot_ids = my_col * slot_count + jnp.arange(slot_count, dtype=jnp.int32)
    own_blocks = my_row * block_rows + jnp.arange(block_rows, dtype=jnp.int32)
    peer_row = (pattern // block_rows).reshape(tile_count)
    order_key = (
        slot_ids[None, :] * all_blocks + jnp.minimum(own_blocks[:, None], pattern)
    ).reshape(tile_count)
    same_peer = peer_row[:, None] == peer_row[None, :]
    before = order_key[None, :] < order_key[:, None]
    peer_rank = jnp.sum((same_peer & before).astype(jnp.int32), axis=1)
    dest_slot = peer_row * capacity + peer_rank
    source_row = jnp.arange(tile_count, dtype=jnp.int32) // slot_count

    def pack_slots(values):
        empty_slots = jnp.zeros((row_count * capacity,) + values.shape[1:], jnp.float32)
        return empty_slots.at[dest_slot].set(values)

    def unpack_slots(received):
        return received[dest_slot].reshape((block_rows, slot_count) + received.shape[1:])

    x_tiles = unpack_slots(
        lax.all_to_all(
            pack_slots(x_blocks[source_row]), "row", split_axis=0, concat_axis=0, tiled=True
        )
    )
    first_diag = my_col * diag_blocks
    x_diag = lax.dynamic_slice_in_dim(x_blocks, first_diag, diag_blocks, 0)
    identity = jnp.eye(block_size, dtype=jnp.float32)
    tile_vals = omega_tiles
    diag_vals = omega_diag.reshape(diag_blocks, block_size, block_size)
    for sweep_index in range(ITERS):
        row_terms = jnp.einsum("askm,asmn->akn", tile_vals, x_tiles, precision=highest)
        diag_terms = jnp.einsum("bkm,bmn->bkn", diag_vals, x_diag, precision=highest)
        own_terms = lax.dynamic_slice_in_dim(row_terms, first_diag, diag_blocks, 0) + diag_terms
        row_terms = lax.dynamic_update_slice_in_dim(row_terms, own_terms, first_diag, 0)
        products = lax.psum(row_terms, "col")
        cross_terms = jnp.einsum("akn,asqn->askq", products, x_tiles, precision=highest)
        returned = lax.all_to_all(
            pack_slots(products[source_row]), "row", split_axis=0, concat_axis=0, tiled=True
        )
        mirror = jnp.einsum("akn,asqn->askq", x_blocks, unpack_slots(returned), precision=highest)
        gradient = (cross_terms + mirror) * (0.5 / sample_count) + ridge_weight * tile_vals
        tile_vals = soft_shrink(tile_vals - step_size * gradient, step_size * shrink_weight)
        y_diag = lax.dynamic_slice_in_dim(products, first_diag, diag_blocks, 0)
        self_cross = jnp.einsum("bkn,bqn->bkq", y_diag, x_diag, precision=highest)
        pivots = jnp.diagonal(diag_vals, axis1=1, axis2=2)
        diag_grad = (self_cross + jnp.swapaxes(self_cross, 1, 2)) * (
            0.5 / sample_count
        ) + ridge_weight * diag_vals
        diag_grad = diag_grad - identity * (1.0 / pivots)[:, :, None]
        stepped = diag_vals - step_size * diag_grad
        diag_vals = identity * stepped + (1.0 - identity) * soft_shrink(
            stepped, step_size * shrink_weight
        )
    return (tile_vals, diag_vals.reshape(omega_diag.shape))


def halves(values):
    high = values.astype(jnp.bfloat16)
    low = (values - high.astype(jnp.float32)).astype(jnp.bfloat16)
    return high, low


def stacked(values):
    return jnp.concatenate(halves(values), axis=0)


def beside(values):
    return jnp.concatenate(halves(values), axis=1)


def fold(full):
    rows, cols = full.shape[0] // 2, full.shape[1] // 2
    return full[:rows, :cols] + (full[:rows, cols:] + full[rows:, :cols])


def times(left, right):
    return jnp.dot(stacked(left), beside(right), preferred_element_type=jnp.float32)


def doubled(values):
    tall = stacked(values)
    return jnp.concatenate([tall, tall], axis=1)


def times_transposed(left_doubled, rights):
    right = jnp.concatenate([beside(r) for r in rights], axis=0)
    full = lax.dot_general(
        left_doubled, right, (((1,), (1,)), ((), ())), preferred_element_type=jnp.float32
    )
    rows, cols = full.shape[0] // 2, rights[0].shape[0]
    full = full[:rows] + full[rows:]
    return [full[:, n * cols : (n + 1) * cols] for n in range(len(rights))]


def product_row(tile_of, x_of, slot_count):
    left = jnp.concatenate([tile_of(s) for s in range(slot_count)], axis=1)
    right = jnp.concatenate([x_of(s) for s in range(slot_count)], axis=0)
    return fold(times(left, right))


def stepped_diag(diag, pair_sum, sample_count):
    size = diag.shape[0]
    on_diagonal = lax.broadcasted_iota(jnp.int32, (size, size), 0) == lax.broadcasted_iota(
        jnp.int32, (size, size), 1
    )
    gradient = pair_sum * (0.5 / sample_count) + ridge_weight * diag
    gradient = gradient - jnp.where(on_diagonal, 1.0 / jnp.where(on_diagonal, diag, 1.0), 0.0)
    stepped = diag - step_size * gradient
    return jnp.where(on_diagonal, stepped, soft_shrink(stepped, step_size * shrink_weight))


MESH = pl.DeviceIdType.MESH
CORNERS = 4
SLOT_GROUP = 2
SEND_US = 1.44
HOP_US = 1.7
LEAD_US = 2.5
ROW_US = (0.42, 0.85)
UNIT_US = 1.44
INNER, OUTER, ACROSS_X, ACROSS_Y, PARTNER = range(5)


class Place:
    def __init__(self):
        self.row = lax.axis_index("row")
        self.col = lax.axis_index("col")
        self.planes = lax.axis_size("row") // CORNERS
        z = self.row // CORNERS
        corner = self.row % CORNERS
        y, x = corner // 2, corner % 2
        upper = (z >= self.planes // 2).astype(jnp.int32)
        self.sign = 1 - 2 * upper
        self.base = upper * (self.planes - 1)
        self.plane = self.base + self.sign * z
        self.corners = {
            "own": corner,
            "beside": y * 2 + (1 - x),
            "across": (1 - y) * 2 + x,
            "opposite": (1 - y) * 2 + (1 - x),
        }
        first = z * CORNERS
        self.target = {
            INNER: (self.row + CORNERS * self.sign, self.col),
            OUTER: (self.row - CORNERS * self.sign, self.col),
            ACROSS_X: (first + self.corners["beside"], self.col),
            ACROSS_Y: (first + self.corners["across"], self.col),
            PARTNER: (self.row, 1 - self.col),
        }

    def source(self, origin, corner):
        return (self.base + self.sign * origin) * CORNERS + self.corners[corner]


def in_plane(planes, plane, origin):
    middle = planes // 2
    if plane < middle:
        return plane <= origin < middle
    return middle <= origin <= plane


def onward(planes, plane, origin, corner, part):
    found = []
    rising = origin <= plane < planes - 1
    falling = origin >= plane > 0
    if corner == "own":
        if rising:
            found.append((INNER, plane + 1, "own"))
        if falling:
            found.append((OUTER, plane - 1, "own"))
        found += [(ACROSS_X, plane, "beside"), (ACROSS_Y, plane, "across")]
    elif corner == "beside":
        if in_plane(planes, plane, origin) and part % 2 == 1:
            found.append((ACROSS_Y, plane, "opposite"))
    elif corner == "across":
        if in_plane(planes, plane, origin) and part % 2 == 0:
            found.append((ACROSS_X, plane, "opposite"))
    else:
        if rising and not in_plane(planes, plane + 1, origin):
            found.append((INNER, plane + 1, "opposite"))
        if falling and not in_plane(planes, plane - 1, origin):
            found.append((OUTER, plane - 1, "opposite"))
    return found


def plan(planes, ready):
    parts = len(ready)
    waiting = {}
    free_at = {}
    acts = [[] for _ in range(planes)]
    events = []
    count = 0
    for plane in range(planes):
        for q in range(parts):
            events.append((ready[q], count, plane, (plane, "own", q), None))
            count += 1
    while events:
        event = min(events)
        events.remove(event)
        now, _, plane, part, link = event
        touched = []
        if link is None:
            origin, corner, q = part
            if (origin, corner) != (plane, "own"):
                acts[plane].append((now, "take", part))
            for out, _, _ in onward(planes, plane, origin, corner, q):
                waiting.setdefault((plane, out), []).append(
                    (abs(plane - origin), now, count, part)
                )
                count += 1
                touched.append((plane, out))
        else:
            touched.append((plane, link))
        for key in touched:
            queue = waiting.get(key, [])
            if not queue or free_at.get(key, -1.0) > now:
                continue
            item = min(queue)
            queue.remove(item)
            free_at[key] = now + SEND_US
            events.append((now + SEND_US, count, plane, None, key[1]))
            count += 1
            sent = item[3]
            if sent[:2] != (plane, "own"):
                acts[plane].append((max(item[1], now - LEAD_US) + 1e-6, "send", key[1], sent))
            for out, to, corner in onward(planes, plane, *sent):
                if out == key[1]:
                    events.append(
                        (now + SEND_US + HOP_US, count, to, (sent[0], corner, sent[2]), None)
                    )
                    count += 1
    return [sorted(found, key=lambda act: act[0]) for found in acts]


class Gather:
    def __init__(self, place, all_ref, parts, recv, passed, met, sent, ready):
        self.place, self.all_ref, self.parts = place, all_ref, parts
        self.recv, self.passed, self.met, self.sent = recv, passed, met, sent
        self.size = all_ref.shape[0] // (place.planes * CORNERS * 2 * parts)
        self.near = range((place.planes + 1) // 2)
        self.acts = plan(place.planes, ready)

    def copy(self, link, part, col=None):
        origin, corner, q = part
        row = self.place.source(origin, corner)
        col = self.place.col if col is None else col
        ref = self.all_ref.at[pl.ds(((row * 2 + col) * self.parts + q) * self.size, self.size)]
        landed = self.recv.at[row, q] if link != PARTNER else self.passed
        return self.describe(ref, link, landed)

    def describe(self, ref, link, landed):
        return pltpu.make_async_remote_copy(
            src_ref=ref,
            dst_ref=ref,
            send_sem=self.sent.at[link],
            recv_sem=landed,
            device_id=self.place.target[link],
            device_id_type=MESH,
        )

    def own(self, q, col=None):
        col = self.place.col if col is None else col
        first = ((self.place.row * 2 + col) * self.parts + q) * self.size
        return self.all_ref.at[pl.ds(first, self.size)]

    def start_own(self, q):
        ref = self.own(q)
        for link in (ACROSS_X, ACROSS_Y, INNER):
            self.describe(ref, link, self.recv.at[self.place.row, q]).start()

        @pl.when(self.place.plane > 0)
        def _():
            self.describe(ref, OUTER, self.recv.at[self.place.row, q]).start()

        self.describe(ref, PARTNER, self.met.at[q]).start()

    def meet(self, q):
        self.describe(self.own(q, 1 - self.place.col), PARTNER, self.met.at[q]).wait_recv()

    def run(self, after, until):
        for plane in self.near:
            chosen = [act for act in self.acts[plane] if after < act[0] <= until]
            if chosen:

                @pl.when(self.place.plane == plane)
                def _(chosen=chosen):
                    for act in chosen:
                        if act[1] == "take":
                            self.copy(INNER, act[2]).wait_recv()
                            self.copy(PARTNER, act[2]).start()
                        else:
                            self.copy(act[2], act[3]).start()

    def all_passed(self):
        count = (self.place.planes * CORNERS - 1) * self.parts * self.size
        self.describe(self.all_ref.at[pl.ds(0, count)], PARTNER, self.passed).wait_recv()

    def all_sent(self):
        for plane in self.near:

            @pl.when(self.place.plane == plane)
            def _(plane=plane):
                counts = [0] * 5
                for act in self.acts[plane]:
                    counts[PARTNER if act[1] == "take" else act[2]] += 1
                for link in range(5):
                    own = self.parts if link != OUTER or plane > 0 else 0
                    total = (counts[link] + own) * self.size
                    if total:
                        ref = self.all_ref.at[pl.ds(0, total)]
                        self.describe(ref, link, self.passed).wait_send()


def greet(place):
    barrier = pltpu.get_barrier_semaphore()
    for link in (ACROSS_X, ACROSS_Y, PARTNER, INNER):
        pl.semaphore_signal(barrier, inc=1, device_id=place.target[link], device_id_type=MESH)

    @pl.when(place.plane > 0)
    def _():
        pl.semaphore_signal(barrier, inc=1, device_id=place.target[OUTER], device_id_type=MESH)

    pl.semaphore_wait(barrier, 4 + (place.plane > 0).astype(jnp.int32))


def slot_groups(slot_count):
    return [range(s, min(s + SLOT_GROUP, slot_count)) for s in range(0, slot_count, SLOT_GROUP)]


def mirror_row(a, first_own, pattern, tiles, x_all, y_all, stepped, sample_count):
    slot_count = tiles.shape[1]
    pair_weight = step_size * 0.5 / sample_count
    left = doubled(x_all[first_own + a])
    for group in slot_groups(slot_count):
        found = times_transposed(left, [y_all[pattern[a, s]] for s in group])
        for s, mirror in zip(group, found):
            stepped[a, s] = soft_shrink(
                tiles[a, s] - pair_weight * mirror, step_size * shrink_weight
            )


def sweeps_kernel(
    pattern_in,
    tiles_in,
    diag_in,
    samples,
    tiles,
    x_all,
    y_last,
    diag,
    pattern,
    y_part,
    y_in,
    recv,
    passed,
    met,
    sent,
    local,
    pair,
    *y_before,
):
    place = Place()
    y_every = [*y_before, y_last]
    block_rows, slot_count = tiles.shape[:2]
    diag_blocks = diag_in.shape[0]
    sample_count = x_all.shape[2]
    first_own = place.row * block_rows
    first_diag = place.col * diag_blocks
    first_other = (1 - place.col) * diag_blocks
    load = pltpu.make_async_copy(tiles_in, tiles, local.at[0])
    load_diag = pltpu.make_async_copy(diag_in, diag, local.at[2])
    load_pattern = pltpu.make_async_copy(pattern_in, pattern, local.at[3])
    mine = pl.ds(first_own + first_diag, diag_blocks)
    take = pltpu.make_async_copy(samples, x_all.at[mine], local.at[1])
    take.start()
    load.start()
    load_diag.start()
    load_pattern.start()

    def gather(n, all_ref, ready):
        return Gather(
            place, all_ref, diag_blocks, recv.at[n % 2], passed.at[n % 2], met.at[n % 2], sent.at[n], ready
        )

    forever = float("inf")
    gathers = [gather(0, x_all, [0.0] * diag_blocks)]
    greet(place)
    take.wait()
    for q in range(diag_blocks):
        gathers[0].start_own(q)
    gathers[0].run(-1.0, forever)
    for q in range(diag_blocks):
        gathers[0].meet(q)
    gathers[0].all_passed()
    load.wait()
    load_diag.wait()
    load_pattern.wait()

    def y_row(a):
        y_part[a] = product_row(lambda s: tiles[a, s], lambda s: x_all[pattern[a, s]], slot_count)

    def send_partial(sweep, d):
        return pltpu.make_async_remote_copy(
            src_ref=y_part.at[first_other + d],
            dst_ref=y_in.at[sweep, d],
            send_sem=pair.at[0, sweep, d],
            recv_sem=pair.at[1, sweep, d],
            device_id=place.target[PARTNER],
            device_id_type=MESH,
        )

    groups = slot_groups(slot_count)
    pair_weight = step_size * 0.5 / sample_count

    def cross_tiles(a, y_all):
        left = doubled(y_all[first_own + a])
        for group in groups:
            found = times_transposed(left, [x_all[pattern[a, s]] for s in group])
            for s, cross in zip(group, found):
                tiles[a, s] = (1.0 - step_size * ridge_weight) * tiles[a, s] - pair_weight * cross

    def mirror_tiles(a, y_all):
        mirror_row(a, first_own, pattern, tiles, x_all, y_all, tiles, sample_count)

    def step_own(d, y_all):
        own = first_own + first_diag + d
        pair_sum = (
            times_transposed(doubled(y_all[own]), [x_all[own]])[0]
            + times_transposed(doubled(x_all[own]), [y_all[own]])[0]
        )
        diag[d] = stepped_diag(diag[d], pair_sum, sample_count)

    def products(sweep, before):
        y_all = y_every[sweep]
        row_us = ROW_US[min(sweep, 1)]
        ready = [2 * row_us * d for d in range(diag_blocks)]
        going = gather(1 + sweep, y_all, ready)
        gathers.append(going)

        def finalize(d):
            send_partial(sweep, d).wait()
            y_all[first_own + first_diag + d] = y_part[first_diag + d] + y_in[sweep, d]
            going.start_own(d)

        @pl.loop(0, diag_blocks)
        def _(d):
            before(first_other + d)
            y_row(first_other + d)
            send_partial(sweep, d).start()

            if sweep == 0:

                @pl.when(d > 0)
                def _():
                    finalize(d - 1)

            for k in range(1, diag_blocks):

                @pl.when(d == k)
                def _(k=k):
                    going.run(ready[k - 1] - 2 * row_us, ready[k - 1])

            before(first_diag + d)
            y_row(first_diag + d)
            y_part[first_diag + d] += fold(times(diag[d], x_all[first_own + first_diag + d]))
            if sweep:
                finalize(d)

        if sweep == 0:
            finalize(diag_blocks - 1)

        @pl.loop(0, block_rows)
        def _(n):
            for k in range(block_rows):

                @pl.when(n == k)
                def _(k=k):
                    if k == diag_blocks:
                        for q in range(diag_blocks):
                            going.meet(q)
                    begin = ready[-1] + k * UNIT_US
                    going.run(ready[-2] if k == 0 else begin - UNIT_US, begin)

            cross_tiles((first_diag + n) % block_rows, y_all)

            @pl.when(n < diag_blocks)
            def _():
                step_own(n, y_all)

        going.run(ready[-1] + (block_rows - 1) * UNIT_US, forever)
        going.all_passed()

    products(0, lambda a: None)
    for sweep in range(1, ITERS):
        products(sweep, lambda a: mirror_tiles(a, y_every[sweep - 1]))
    for done in gathers:
        done.all_sent()


def finish_kernel(pattern, tiles, x_all, y_all, diag_in, tiles_out, diag_out, ready, sems):
    block_rows, slot_count = tiles.shape[:2]
    sample_count = x_all.shape[2]
    first_own = lax.axis_index("row") * block_rows
    store_diag = pltpu.make_async_copy(diag_in, diag_out, sems.at[block_rows])
    store_diag.start()

    def store(a):
        return pltpu.make_async_copy(ready.at[a], tiles_out.at[a], sems.at[a])

    @pl.loop(0, block_rows)
    def _(a):
        mirror_row(a, first_own, pattern, tiles, x_all, y_all, ready, sample_count)
        store(a).start()

    store_diag.wait()

    @pl.loop(0, block_rows)
    def _(a):
        store(a).wait()


def gathered_sweeps(omega_tiles, omega_diag, samples, pattern):
    block_rows, slot_count, size, _ = omega_tiles.shape
    row_count = lax.axis_size("row")
    sample_count = samples.shape[1]
    diag_blocks = block_rows // lax.axis_size("col")
    diag = omega_diag.reshape(diag_blocks, size, size)
    every = (row_count * block_rows, size, sample_count)
    in_vmem = pl.BlockSpec(memory_space=pltpu.VMEM)
    in_hbm = pl.BlockSpec(memory_space=pltpu.HBM)
    in_smem = pl.BlockSpec(memory_space=pltpu.SMEM)
    tiles, x_all, y_all, diag, listed = pl.pallas_call(
        sweeps_kernel,
        name="sweeps",
        out_shape=[
            pltpu.VMEM(omega_tiles.shape, jnp.float32),
            pltpu.VMEM(every, jnp.float32),
            pltpu.VMEM(every, jnp.float32),
            pltpu.VMEM(diag.shape, jnp.float32),
            pltpu.SMEM(pattern.shape, jnp.int32),
        ],
        in_specs=[in_hbm] * 4,
        out_specs=[in_vmem] * 4 + [in_smem],
        scratch_shapes=[
            pltpu.VMEM((block_rows, size, sample_count), jnp.float32),
            pltpu.VMEM((ITERS, diag_blocks, size, sample_count), jnp.float32),
            pltpu.SemaphoreType.DMA((2, row_count, diag_blocks)),
            pltpu.SemaphoreType.DMA((2,)),
            pltpu.SemaphoreType.DMA((2, diag_blocks)),
            pltpu.SemaphoreType.DMA((1 + ITERS, 5)),
            pltpu.SemaphoreType.DMA((4,)),
            pltpu.SemaphoreType.DMA((2, ITERS, diag_blocks)),
        ]
        + [pltpu.VMEM(every, jnp.float32)] * (ITERS - 1),
        compiler_params=pltpu.CompilerParams(
            collective_id=0, has_side_effects=True, vmem_limit_bytes=40 * 2**20
        ),
    )(
        *(
            pltpu.with_memory_space_constraint(v, pltpu.HBM)
            for v in (pattern, omega_tiles, diag, samples.reshape(diag_blocks, size, sample_count))
        ),
    )
    held = [pltpu.with_memory_space_constraint(v, pltpu.VMEM) for v in (tiles, x_all, y_all, diag)]
    tiles, diag = pl.pallas_call(
        finish_kernel,
        name="finish",
        out_shape=[
            jax.ShapeDtypeStruct(omega_tiles.shape, jnp.float32),
            jax.ShapeDtypeStruct(diag.shape, jnp.float32),
        ],
        in_specs=[in_smem] + [in_vmem] * 4,
        out_specs=[in_hbm, in_hbm],
        scratch_shapes=[
            pltpu.VMEM(omega_tiles.shape, jnp.float32),
            pltpu.SemaphoreType.DMA((block_rows + 1,)),
        ],
        compiler_params=pltpu.CompilerParams(vmem_limit_bytes=16 * 2**20),
    )(pltpu.with_memory_space_constraint(listed, pltpu.SMEM), *held)
    return tiles, diag.reshape(omega_diag.shape)


def on_device(omega_tiles, omega_diag, samples, pattern):
    row_count = lax.axis_size("row")
    block_rows, slot_count = omega_tiles.shape[:2]
    peer_span = row_count // 2 - 2
    capacity = max(1, (slot_count * block_rows // 2 - 1 + peer_span - 1) // peer_span)
    whole_gather = 2 * capacity >= block_rows and lax.axis_size("col") == 2 and row_count % 8 == 0
    sweeps = gathered_sweeps if whole_gather else listed_sweeps
    return sweeps(omega_tiles, omega_diag, samples, pattern)


def solution(mesh):
    in_specs = (
        P("row", "col", None, None),
        P(("row", "col"), None),
        P(("row", "col"), None),
        P("row", "col"),
    )
    out_specs = (P("row", "col", None, None), P(("row", "col"), None))
    return jax.shard_map(
        on_device, mesh=mesh, in_specs=in_specs, out_specs=out_specs, check_vma=False
    )
```

```python
import jax
import jax.numpy as jnp
from jax import lax
from jax.experimental import pallas as pl
from jax.experimental.pallas import tpu as pltpu
from jax.sharding import PartitionSpec as P

ITERS = 2


step_size = 0.2
shrink_weight = 0.05
ridge_weight = 0.1


def soft_shrink(values, threshold):
    return values - jnp.clip(values, -threshold, threshold)


def listed_sweeps(omega_tiles, omega_diag, samples, pattern):
    highest = lax.Precision.HIGHEST
    row_count = lax.axis_size("row")
    col_count = lax.axis_size("col")
    my_row = lax.axis_index("row")
    my_col = lax.axis_index("col")
    block_rows = omega_tiles.shape[0]
    slot_count = omega_tiles.shape[1]
    block_size = omega_tiles.shape[2]
    sample_count = samples.shape[1]
    diag_blocks = block_rows // col_count
    all_blocks = block_rows * row_count
    peer_span = row_count // 2 - 2
    capacity = max(1, (slot_count * block_rows // 2 - 1 + peer_span - 1) // peer_span)
    tile_count = block_rows * slot_count
    x_rows = lax.all_gather(samples, "col", axis=0, tiled=True)
    x_blocks = x_rows.reshape(block_rows, block_size, sample_count)
    slot_ids = my_col * slot_count + jnp.arange(slot_count, dtype=jnp.int32)
    own_blocks = my_row * block_rows + jnp.arange(block_rows, dtype=jnp.int32)
    peer_row = (pattern // block_rows).reshape(tile_count)
    order_key = (
        slot_ids[None, :] * all_blocks + jnp.minimum(own_blocks[:, None], pattern)
    ).reshape(tile_count)
    same_peer = peer_row[:, None] == peer_row[None, :]
    before = order_key[None, :] < order_key[:, None]
    peer_rank = jnp.sum((same_peer & before).astype(jnp.int32), axis=1)
    dest_slot = peer_row * capacity + peer_rank
    source_row = jnp.arange(tile_count, dtype=jnp.int32) // slot_count

    def pack_slots(values):
        empty_slots = jnp.zeros((row_count * capacity,) + values.shape[1:], jnp.float32)
        return empty_slots.at[dest_slot].set(values)

    def unpack_slots(received):
        return received[dest_slot].reshape((block_rows, slot_count) + received.shape[1:])

    x_tiles = unpack_slots(
        lax.all_to_all(
            pack_slots(x_blocks[source_row]), "row", split_axis=0, concat_axis=0, tiled=True
        )
    )
    first_diag = my_col * diag_blocks
    x_diag = lax.dynamic_slice_in_dim(x_blocks, first_diag, diag_blocks, 0)
    identity = jnp.eye(block_size, dtype=jnp.float32)
    tile_vals = omega_tiles
    diag_vals = omega_diag.reshape(diag_blocks, block_size, block_size)
    for sweep_index in range(ITERS):
        row_terms = jnp.einsum("askm,asmn->akn", tile_vals, x_tiles, precision=highest)
        diag_terms = jnp.einsum("bkm,bmn->bkn", diag_vals, x_diag, precision=highest)
        own_terms = lax.dynamic_slice_in_dim(row_terms, first_diag, diag_blocks, 0) + diag_terms
        row_terms = lax.dynamic_update_slice_in_dim(row_terms, own_terms, first_diag, 0)
        products = lax.psum(row_terms, "col")
        cross_terms = jnp.einsum("akn,asqn->askq", products, x_tiles, precision=highest)
        returned = lax.all_to_all(
            pack_slots(products[source_row]), "row", split_axis=0, concat_axis=0, tiled=True
        )
        mirror = jnp.einsum("akn,asqn->askq", x_blocks, unpack_slots(returned), precision=highest)
        gradient = (cross_terms + mirror) * (0.5 / sample_count) + ridge_weight * tile_vals
        tile_vals = soft_shrink(tile_vals - step_size * gradient, step_size * shrink_weight)
        y_diag = lax.dynamic_slice_in_dim(products, first_diag, diag_blocks, 0)
        self_cross = jnp.einsum("bkn,bqn->bkq", y_diag, x_diag, precision=highest)
        pivots = jnp.diagonal(diag_vals, axis1=1, axis2=2)
        diag_grad = (self_cross + jnp.swapaxes(self_cross, 1, 2)) * (
            0.5 / sample_count
        ) + ridge_weight * diag_vals
        diag_grad = diag_grad - identity * (1.0 / pivots)[:, :, None]
        stepped = diag_vals - step_size * diag_grad
        diag_vals = identity * stepped + (1.0 - identity) * soft_shrink(
            stepped, step_size * shrink_weight
        )
    return (tile_vals, diag_vals.reshape(omega_diag.shape))


def halves(values):
    high = values.astype(jnp.bfloat16)
    low = (values - high.astype(jnp.float32)).astype(jnp.bfloat16)
    return high, low


def stacked(values):
    return jnp.concatenate(halves(values), axis=0)


def beside(values):
    return jnp.concatenate(halves(values), axis=1)


def fold(full):
    rows, cols = full.shape[0] // 2, full.shape[1] // 2
    return full[:rows, :cols] + (full[:rows, cols:] + full[rows:, :cols])


def times(left, right):
    return jnp.dot(stacked(left), beside(right), preferred_element_type=jnp.float32)


def doubled(values):
    tall = stacked(values)
    return jnp.concatenate([tall, tall], axis=1)


def times_transposed(left_doubled, rights):
    right = jnp.concatenate([beside(r) for r in rights], axis=0)
    full = lax.dot_general(
        left_doubled, right, (((1,), (1,)), ((), ())), preferred_element_type=jnp.float32
    )
    rows, cols = full.shape[0] // 2, rights[0].shape[0]
    full = full[:rows] + full[rows:]
    return [full[:, n * cols : (n + 1) * cols] for n in range(len(rights))]


def product_row(tile_of, x_of, slot_count):
    left = jnp.concatenate([tile_of(s) for s in range(slot_count)], axis=1)
    right = jnp.concatenate([x_of(s) for s in range(slot_count)], axis=0)
    return fold(times(left, right))


def stepped_diag(diag, pair_sum, sample_count):
    size = diag.shape[0]
    on_diagonal = lax.broadcasted_iota(jnp.int32, (size, size), 0) == lax.broadcasted_iota(
        jnp.int32, (size, size), 1
    )
    gradient = pair_sum * (0.5 / sample_count) + ridge_weight * diag
    gradient = gradient - jnp.where(on_diagonal, 1.0 / jnp.where(on_diagonal, diag, 1.0), 0.0)
    stepped = diag - step_size * gradient
    return jnp.where(on_diagonal, stepped, soft_shrink(stepped, step_size * shrink_weight))


MESH = pl.DeviceIdType.MESH
CORNERS = 4
SLOT_GROUP = 2
SEND_US = 1.44
HOP_US = 1.7
LEAD_US = 2.5
ROW_US = (0.42, 0.85)
UNIT_US = 1.44
INNER, OUTER, ACROSS_X, ACROSS_Y, PARTNER = range(5)


class Place:
    def __init__(self):
        self.row = lax.axis_index("row")
        self.col = lax.axis_index("col")
        self.planes = lax.axis_size("row") // CORNERS
        z = self.row // CORNERS
        corner = self.row % CORNERS
        y, x = corner // 2, corner % 2
        upper = (z >= self.planes // 2).astype(jnp.int32)
        self.sign = 1 - 2 * upper
        self.base = upper * (self.planes - 1)
        self.plane = self.base + self.sign * z
        self.corners = {
            "own": corner,
            "beside": y * 2 + (1 - x),
            "across": (1 - y) * 2 + x,
            "opposite": (1 - y) * 2 + (1 - x),
        }
        first = z * CORNERS
        self.target = {
            INNER: (self.row + CORNERS * self.sign, self.col),
            OUTER: (self.row - CORNERS * self.sign, self.col),
            ACROSS_X: (first + self.corners["beside"], self.col),
            ACROSS_Y: (first + self.corners["across"], self.col),
            PARTNER: (self.row, 1 - self.col),
        }

    def source(self, origin, corner):
        return (self.base + self.sign * origin) * CORNERS + self.corners[corner]


def in_plane(planes, plane, origin):
    middle = planes // 2
    if plane < middle:
        return plane <= origin < middle
    return middle <= origin <= plane


def onward(planes, plane, origin, corner, part):
    found = []
    rising = origin <= plane < planes - 1
    falling = origin >= plane > 0
    if corner == "own":
        if rising:
            found.append((INNER, plane + 1, "own"))
        if falling:
            found.append((OUTER, plane - 1, "own"))
        found += [(ACROSS_X, plane, "beside"), (ACROSS_Y, plane, "across")]
    elif corner == "beside":
        if in_plane(planes, plane, origin) and part % 2 == 1:
            found.append((ACROSS_Y, plane, "opposite"))
    elif corner == "across":
        if in_plane(planes, plane, origin) and part % 2 == 0:
            found.append((ACROSS_X, plane, "opposite"))
    else:
        if rising and not in_plane(planes, plane + 1, origin):
            found.append((INNER, plane + 1, "opposite"))
        if falling and not in_plane(planes, plane - 1, origin):
            found.append((OUTER, plane - 1, "opposite"))
    return found


def plan(planes, ready):
    parts = len(ready)
    waiting = {}
    free_at = {}
    acts = [[] for _ in range(planes)]
    events = []
    count = 0
    for plane in range(planes):
        for q in range(parts):
            events.append((ready[q], count, plane, (plane, "own", q), None))
            count += 1
    while events:
        event = min(events)
        events.remove(event)
        now, _, plane, part, link = event
        touched = []
        if link is None:
            origin, corner, q = part
            if (origin, corner) != (plane, "own"):
                acts[plane].append((now, "take", part))
            for out, _, _ in onward(planes, plane, origin, corner, q):
                waiting.setdefault((plane, out), []).append(
                    (abs(plane - origin), now, count, part)
                )
                count += 1
                touched.append((plane, out))
        else:
            touched.append((plane, link))
        for key in touched:
            queue = waiting.get(key, [])
            if not queue or free_at.get(key, -1.0) > now:
                continue
            item = min(queue)
            queue.remove(item)
            free_at[key] = now + SEND_US
            events.append((now + SEND_US, count, plane, None, key[1]))
            count += 1
            sent = item[3]
            if sent[:2] != (plane, "own"):
                acts[plane].append((max(item[1], now - LEAD_US) + 1e-6, "send", key[1], sent))
            for out, to, corner in onward(planes, plane, *sent):
                if out == key[1]:
                    events.append(
                        (now + SEND_US + HOP_US, count, to, (sent[0], corner, sent[2]), None)
                    )
                    count += 1
    return [sorted(found, key=lambda act: act[0]) for found in acts]


class Gather:
    def __init__(self, place, all_ref, parts, recv, passed, met, sent, ready):
        self.place, self.all_ref, self.parts = place, all_ref, parts
        self.recv, self.passed, self.met, self.sent = recv, passed, met, sent
        self.size = all_ref.shape[0] // (place.planes * CORNERS * 2 * parts)
        self.near = range((place.planes + 1) // 2)
        self.acts = plan(place.planes, ready)

    def copy(self, link, part, col=None):
        origin, corner, q = part
        row = self.place.source(origin, corner)
        col = self.place.col if col is None else col
        ref = self.all_ref.at[pl.ds(((row * 2 + col) * self.parts + q) * self.size, self.size)]
        landed = self.recv.at[row, q] if link != PARTNER else self.passed
        return self.describe(ref, link, landed)

    def describe(self, ref, link, landed):
        return pltpu.make_async_remote_copy(
            src_ref=ref,
            dst_ref=ref,
            send_sem=self.sent.at[link],
            recv_sem=landed,
            device_id=self.place.target[link],
            device_id_type=MESH,
        )

    def own(self, q, col=None):
        col = self.place.col if col is None else col
        first = ((self.place.row * 2 + col) * self.parts + q) * self.size
        return self.all_ref.at[pl.ds(first, self.size)]

    def start_own(self, q):
        ref = self.own(q)
        for link in (ACROSS_X, ACROSS_Y, INNER):
            self.describe(ref, link, self.recv.at[self.place.row, q]).start()

        @pl.when(self.place.plane > 0)
        def _():
            self.describe(ref, OUTER, self.recv.at[self.place.row, q]).start()

        self.describe(ref, PARTNER, self.met.at[q]).start()

    def meet(self, q):
        self.describe(self.own(q, 1 - self.place.col), PARTNER, self.met.at[q]).wait_recv()

    def run(self, after, until):
        for plane in self.near:
            chosen = [act for act in self.acts[plane] if after < act[0] <= until]
            if chosen:

                @pl.when(self.place.plane == plane)
                def _(chosen=chosen):
                    for act in chosen:
                        if act[1] == "take":
                            self.copy(INNER, act[2]).wait_recv()
                            self.copy(PARTNER, act[2]).start()
                        else:
                            self.copy(act[2], act[3]).start()

    def all_passed(self):
        count = (self.place.planes * CORNERS - 1) * self.parts * self.size
        self.describe(self.all_ref.at[pl.ds(0, count)], PARTNER, self.passed).wait_recv()

    def all_sent(self):
        for plane in self.near:

            @pl.when(self.place.plane == plane)
            def _(plane=plane):
                counts = [0] * 5
                for act in self.acts[plane]:
                    counts[PARTNER if act[1] == "take" else act[2]] += 1
                for link in range(5):
                    own = self.parts if link != OUTER or plane > 0 else 0
                    total = (counts[link] + own) * self.size
                    if total:
                        ref = self.all_ref.at[pl.ds(0, total)]
                        self.describe(ref, link, self.passed).wait_send()


def greet(place):
    barrier = pltpu.get_barrier_semaphore()
    for link in (ACROSS_X, ACROSS_Y, PARTNER, INNER):
        pl.semaphore_signal(barrier, inc=1, device_id=place.target[link], device_id_type=MESH)

    @pl.when(place.plane > 0)
    def _():
        pl.semaphore_signal(barrier, inc=1, device_id=place.target[OUTER], device_id_type=MESH)

    pl.semaphore_wait(barrier, 4 + (place.plane > 0).astype(jnp.int32))


def slot_groups(slot_count):
    return [range(s, min(s + SLOT_GROUP, slot_count)) for s in range(0, slot_count, SLOT_GROUP)]


def mirror_row(a, first_own, pattern, tiles, x_all, y_all, stepped, sample_count):
    slot_count = tiles.shape[1]
    pair_weight = step_size * 0.5 / sample_count
    left = doubled(x_all[first_own + a])
    for group in slot_groups(slot_count):
        found = times_transposed(left, [y_all[pattern[a, s]] for s in group])
        for s, mirror in zip(group, found):
            stepped[a, s] = soft_shrink(
                tiles[a, s] - pair_weight * mirror, step_size * shrink_weight
            )


def sweeps_kernel(
    pattern_in,
    tiles_in,
    diag_in,
    samples,
    tiles,
    x_all,
    y_last,
    diag,
    pattern,
    y_part,
    y_in,
    recv,
    passed,
    met,
    sent,
    local,
    pair,
    *y_before,
):
    place = Place()
    y_every = [*y_before, y_last]
    block_rows, slot_count = tiles.shape[:2]
    diag_blocks = diag_in.shape[0]
    sample_count = x_all.shape[2]
    first_own = place.row * block_rows
    first_diag = place.col * diag_blocks
    first_other = (1 - place.col) * diag_blocks
    load = pltpu.make_async_copy(tiles_in, tiles, local.at[0])
    load_diag = pltpu.make_async_copy(diag_in, diag, local.at[2])
    load_pattern = pltpu.make_async_copy(pattern_in, pattern, local.at[3])
    mine = pl.ds(first_own + first_diag, diag_blocks)
    take = pltpu.make_async_copy(samples, x_all.at[mine], local.at[1])
    take.start()
    load.start()
    load_diag.start()
    load_pattern.start()

    def gather(n, all_ref, ready):
        return Gather(
            place, all_ref, diag_blocks, recv.at[n % 2], passed.at[n % 2], met.at[n % 2], sent.at[n], ready
        )

    forever = float("inf")
    gathers = [gather(0, x_all, [0.0] * diag_blocks)]
    greet(place)
    take.wait()
    for q in range(diag_blocks):
        gathers[0].start_own(q)
    gathers[0].run(-1.0, forever)
    for q in range(diag_blocks):
        gathers[0].meet(q)
    gathers[0].all_passed()
    load.wait()
    load_diag.wait()
    load_pattern.wait()

    def y_row(a):
        y_part[a] = product_row(lambda s: tiles[a, s], lambda s: x_all[pattern[a, s]], slot_count)

    def send_partial(sweep, d):
        return pltpu.make_async_remote_copy(
            src_ref=y_part.at[first_other + d],
            dst_ref=y_in.at[sweep, d],
            send_sem=pair.at[0, sweep, d],
            recv_sem=pair.at[1, sweep, d],
            device_id=place.target[PARTNER],
            device_id_type=MESH,
        )

    groups = slot_groups(slot_count)
    pair_weight = step_size * 0.5 / sample_count

    def cross_tiles(a, y_all):
        left = doubled(y_all[first_own + a])
        for group in groups:
            found = times_transposed(left, [x_all[pattern[a, s]] for s in group])
            for s, cross in zip(group, found):
                tiles[a, s] = (1.0 - step_size * ridge_weight) * tiles[a, s] - pair_weight * cross

    def mirror_tiles(a, y_all):
        mirror_row(a, first_own, pattern, tiles, x_all, y_all, tiles, sample_count)

    def step_own(d, y_all):
        own = first_own + first_diag + d
        pair_sum = (
            times_transposed(doubled(y_all[own]), [x_all[own]])[0]
            + times_transposed(doubled(x_all[own]), [y_all[own]])[0]
        )
        diag[d] = stepped_diag(diag[d], pair_sum, sample_count)

    def products(sweep, before):
        y_all = y_every[sweep]
        row_us = ROW_US[min(sweep, 1)]
        ready = [2 * row_us * d for d in range(diag_blocks)]
        going = gather(1 + sweep, y_all, ready)
        gathers.append(going)

        def finalize(d):
            send_partial(sweep, d).wait()
            y_all[first_own + first_diag + d] = y_part[first_diag + d] + y_in[sweep, d]
            going.start_own(d)

        @pl.loop(0, diag_blocks)
        def _(d):
            before(first_other + d)
            y_row(first_other + d)
            send_partial(sweep, d).start()

            if sweep == 0:

                @pl.when(d > 0)
                def _():
                    finalize(d - 1)

            for k in range(1, diag_blocks):

                @pl.when(d == k)
                def _(k=k):
                    going.run(ready[k - 1] - 2 * row_us, ready[k - 1])

            before(first_diag + d)
            y_row(first_diag + d)
            y_part[first_diag + d] += fold(times(diag[d], x_all[first_own + first_diag + d]))
            if sweep:
                finalize(d)

        if sweep == 0:
            finalize(diag_blocks - 1)

        @pl.loop(0, block_rows)
        def _(n):
            for k in range(block_rows):

                @pl.when(n == k)
                def _(k=k):
                    if k == diag_blocks:
                        for q in range(diag_blocks):
                            going.meet(q)
                    begin = ready[-1] + k * UNIT_US
                    going.run(ready[-2] if k == 0 else begin - UNIT_US, begin)

            cross_tiles((first_diag + n) % block_rows, y_all)

            @pl.when(n < diag_blocks)
            def _():
                step_own(n, y_all)

        going.run(ready[-1] + (block_rows - 1) * UNIT_US, forever)
        going.all_passed()

    products(0, lambda a: None)
    for sweep in range(1, ITERS):
        products(sweep, lambda a: mirror_tiles(a, y_every[sweep - 1]))
    for done in gathers:
        done.all_sent()


def finish_kernel(pattern, tiles, x_all, y_all, diag_in, tiles_out, diag_out, ready, sems):
    block_rows, slot_count = tiles.shape[:2]
    sample_count = x_all.shape[2]
    first_own = lax.axis_index("row") * block_rows
    store_diag = pltpu.make_async_copy(diag_in, diag_out, sems.at[block_rows])
    store_diag.start()

    def store(a):
        return pltpu.make_async_copy(ready.at[a], tiles_out.at[a], sems.at[a])

    def rows(first):
        for a in (first, first + 1):
            mirror_row(a, first_own, pattern, tiles, x_all, y_all, ready, sample_count)
            store(a).start()

    pl.loop(0, block_rows, step=2)(rows)

    store_diag.wait()

    @pl.loop(0, block_rows)
    def _(a):
        store(a).wait()


def gathered_sweeps(omega_tiles, omega_diag, samples, pattern):
    block_rows, slot_count, size, _ = omega_tiles.shape
    row_count = lax.axis_size("row")
    sample_count = samples.shape[1]
    diag_blocks = block_rows // lax.axis_size("col")
    diag = omega_diag.reshape(diag_blocks, size, size)
    every = (row_count * block_rows, size, sample_count)
    in_vmem = pl.BlockSpec(memory_space=pltpu.VMEM)
    in_hbm = pl.BlockSpec(memory_space=pltpu.HBM)
    in_smem = pl.BlockSpec(memory_space=pltpu.SMEM)
    tiles, x_all, y_all, diag, listed = pl.pallas_call(
        sweeps_kernel,
        name="sweeps",
        out_shape=[
            pltpu.VMEM(omega_tiles.shape, jnp.float32),
            pltpu.VMEM(every, jnp.float32),
            pltpu.VMEM(every, jnp.float32),
            pltpu.VMEM(diag.shape, jnp.float32),
            pltpu.SMEM(pattern.shape, jnp.int32),
        ],
        in_specs=[in_hbm] * 4,
        out_specs=[in_vmem] * 4 + [in_smem],
        scratch_shapes=[
            pltpu.VMEM((block_rows, size, sample_count), jnp.float32),
            pltpu.VMEM((ITERS, diag_blocks, size, sample_count), jnp.float32),
            pltpu.SemaphoreType.DMA((2, row_count, diag_blocks)),
            pltpu.SemaphoreType.DMA((2,)),
            pltpu.SemaphoreType.DMA((2, diag_blocks)),
            pltpu.SemaphoreType.DMA((1 + ITERS, 5)),
            pltpu.SemaphoreType.DMA((4,)),
            pltpu.SemaphoreType.DMA((2, ITERS, diag_blocks)),
        ]
        + [pltpu.VMEM(every, jnp.float32)] * (ITERS - 1),
        compiler_params=pltpu.CompilerParams(
            collective_id=0, has_side_effects=True, vmem_limit_bytes=40 * 2**20
        ),
    )(
        *(
            pltpu.with_memory_space_constraint(v, pltpu.HBM)
            for v in (pattern, omega_tiles, diag, samples.reshape(diag_blocks, size, sample_count))
        ),
    )
    held = [pltpu.with_memory_space_constraint(v, pltpu.VMEM) for v in (tiles, x_all, y_all, diag)]
    tiles, diag = pl.pallas_call(
        finish_kernel,
        name="finish",
        out_shape=[
            jax.ShapeDtypeStruct(omega_tiles.shape, jnp.float32),
            jax.ShapeDtypeStruct(diag.shape, jnp.float32),
        ],
        in_specs=[in_smem] + [in_vmem] * 4,
        out_specs=[in_hbm, in_hbm],
        scratch_shapes=[
            pltpu.VMEM(omega_tiles.shape, jnp.float32),
            pltpu.SemaphoreType.DMA((block_rows + 1,)),
        ],
        compiler_params=pltpu.CompilerParams(vmem_limit_bytes=16 * 2**20),
    )(pltpu.with_memory_space_constraint(listed, pltpu.SMEM), *held)
    return tiles, diag.reshape(omega_diag.shape)


def on_device(omega_tiles, omega_diag, samples, pattern):
    row_count = lax.axis_size("row")
    block_rows, slot_count = omega_tiles.shape[:2]
    peer_span = row_count // 2 - 2
    capacity = max(1, (slot_count * block_rows // 2 - 1 + peer_span - 1) // peer_span)
    whole_gather = 2 * capacity >= block_rows and lax.axis_size("col") == 2 and row_count % 8 == 0
    sweeps = gathered_sweeps if whole_gather else listed_sweeps
    return sweeps(omega_tiles, omega_diag, samples, pattern)


def solution(mesh):
    in_specs = (
        P("row", "col", None, None),
        P(("row", "col"), None),
        P(("row", "col"), None),
        P("row", "col"),
    )
    out_specs = (P("row", "col", None, None), P(("row", "col"), None))
    return jax.shard_map(
        on_device, mesh=mesh, in_specs=in_specs, out_specs=out_specs, check_vma=False
    )
```

```python
import jax
import jax.numpy as jnp
from jax import lax
from jax.experimental import pallas as pl
from jax.experimental.pallas import tpu as pltpu
from jax.sharding import PartitionSpec as P

ITERS = 2


step_size = 0.2
shrink_weight = 0.05
ridge_weight = 0.1


def soft_shrink(values, threshold):
    return values - jnp.clip(values, -threshold, threshold)


def listed_sweeps(omega_tiles, omega_diag, samples, pattern):
    highest = lax.Precision.HIGHEST
    row_count = lax.axis_size("row")
    col_count = lax.axis_size("col")
    my_row = lax.axis_index("row")
    my_col = lax.axis_index("col")
    block_rows = omega_tiles.shape[0]
    slot_count = omega_tiles.shape[1]
    block_size = omega_tiles.shape[2]
    sample_count = samples.shape[1]
    diag_blocks = block_rows // col_count
    all_blocks = block_rows * row_count
    peer_span = row_count // 2 - 2
    capacity = max(1, (slot_count * block_rows // 2 - 1 + peer_span - 1) // peer_span)
    tile_count = block_rows * slot_count
    x_rows = lax.all_gather(samples, "col", axis=0, tiled=True)
    x_blocks = x_rows.reshape(block_rows, block_size, sample_count)
    slot_ids = my_col * slot_count + jnp.arange(slot_count, dtype=jnp.int32)
    own_blocks = my_row * block_rows + jnp.arange(block_rows, dtype=jnp.int32)
    peer_row = (pattern // block_rows).reshape(tile_count)
    order_key = (
        slot_ids[None, :] * all_blocks + jnp.minimum(own_blocks[:, None], pattern)
    ).reshape(tile_count)
    same_peer = peer_row[:, None] == peer_row[None, :]
    before = order_key[None, :] < order_key[:, None]
    peer_rank = jnp.sum((same_peer & before).astype(jnp.int32), axis=1)
    dest_slot = peer_row * capacity + peer_rank
    source_row = jnp.arange(tile_count, dtype=jnp.int32) // slot_count

    def pack_slots(values):
        empty_slots = jnp.zeros((row_count * capacity,) + values.shape[1:], jnp.float32)
        return empty_slots.at[dest_slot].set(values)

    def unpack_slots(received):
        return received[dest_slot].reshape((block_rows, slot_count) + received.shape[1:])

    x_tiles = unpack_slots(
        lax.all_to_all(
            pack_slots(x_blocks[source_row]), "row", split_axis=0, concat_axis=0, tiled=True
        )
    )
    first_diag = my_col * diag_blocks
    x_diag = lax.dynamic_slice_in_dim(x_blocks, first_diag, diag_blocks, 0)
    identity = jnp.eye(block_size, dtype=jnp.float32)
    tile_vals = omega_tiles
    diag_vals = omega_diag.reshape(diag_blocks, block_size, block_size)
    for sweep_index in range(ITERS):
        row_terms = jnp.einsum("askm,asmn->akn", tile_vals, x_tiles, precision=highest)
        diag_terms = jnp.einsum("bkm,bmn->bkn", diag_vals, x_diag, precision=highest)
        own_terms = lax.dynamic_slice_in_dim(row_terms, first_diag, diag_blocks, 0) + diag_terms
        row_terms = lax.dynamic_update_slice_in_dim(row_terms, own_terms, first_diag, 0)
        products = lax.psum(row_terms, "col")
        cross_terms = jnp.einsum("akn,asqn->askq", products, x_tiles, precision=highest)
        returned = lax.all_to_all(
            pack_slots(products[source_row]), "row", split_axis=0, concat_axis=0, tiled=True
        )
        mirror = jnp.einsum("akn,asqn->askq", x_blocks, unpack_slots(returned), precision=highest)
        gradient = (cross_terms + mirror) * (0.5 / sample_count) + ridge_weight * tile_vals
        tile_vals = soft_shrink(tile_vals - step_size * gradient, step_size * shrink_weight)
        y_diag = lax.dynamic_slice_in_dim(products, first_diag, diag_blocks, 0)
        self_cross = jnp.einsum("bkn,bqn->bkq", y_diag, x_diag, precision=highest)
        pivots = jnp.diagonal(diag_vals, axis1=1, axis2=2)
        diag_grad = (self_cross + jnp.swapaxes(self_cross, 1, 2)) * (
            0.5 / sample_count
        ) + ridge_weight * diag_vals
        diag_grad = diag_grad - identity * (1.0 / pivots)[:, :, None]
        stepped = diag_vals - step_size * diag_grad
        diag_vals = identity * stepped + (1.0 - identity) * soft_shrink(
            stepped, step_size * shrink_weight
        )
    return (tile_vals, diag_vals.reshape(omega_diag.shape))


def halves(values):
    high = values.astype(jnp.bfloat16)
    low = (values - high.astype(jnp.float32)).astype(jnp.bfloat16)
    return high, low


def stacked(values):
    return jnp.concatenate(halves(values), axis=0)


def beside(values):
    return jnp.concatenate(halves(values), axis=1)


def fold(full):
    rows, cols = full.shape[0] // 2, full.shape[1] // 2
    return full[:rows, :cols] + (full[:rows, cols:] + full[rows:, :cols])


def times(left, right):
    return jnp.dot(stacked(left), beside(right), preferred_element_type=jnp.float32)


def doubled(values):
    tall = stacked(values)
    return jnp.concatenate([tall, tall], axis=1)


def times_transposed(left_doubled, rights):
    right = jnp.concatenate([beside(r) for r in rights], axis=0)
    full = lax.dot_general(
        left_doubled, right, (((1,), (1,)), ((), ())), preferred_element_type=jnp.float32
    )
    rows, cols = full.shape[0] // 2, rights[0].shape[0]
    full = full[:rows] + full[rows:]
    return [full[:, n * cols : (n + 1) * cols] for n in range(len(rights))]


def product_row(tile_of, x_of, slot_count):
    left = jnp.concatenate([tile_of(s) for s in range(slot_count)], axis=1)
    right = jnp.concatenate([x_of(s) for s in range(slot_count)], axis=0)
    return fold(times(left, right))


def stepped_diag(diag, pair_sum, sample_count):
    size = diag.shape[0]
    on_diagonal = lax.broadcasted_iota(jnp.int32, (size, size), 0) == lax.broadcasted_iota(
        jnp.int32, (size, size), 1
    )
    gradient = pair_sum * (0.5 / sample_count) + ridge_weight * diag
    gradient = gradient - jnp.where(on_diagonal, 1.0 / jnp.where(on_diagonal, diag, 1.0), 0.0)
    stepped = diag - step_size * gradient
    return jnp.where(on_diagonal, stepped, soft_shrink(stepped, step_size * shrink_weight))


MESH = pl.DeviceIdType.MESH
CORNERS = 4
SLOT_GROUP = 2
SEND_US = 1.44
HOP_US = 1.7
LEAD_US = 2.5
ROW_US = (0.42, 0.85)
UNIT_US = 1.44
INNER, OUTER, ACROSS_X, ACROSS_Y, PARTNER = range(5)


class Place:
    def __init__(self):
        self.row = lax.axis_index("row")
        self.col = lax.axis_index("col")
        self.planes = lax.axis_size("row") // CORNERS
        z = self.row // CORNERS
        corner = self.row % CORNERS
        y, x = corner // 2, corner % 2
        upper = (z >= self.planes // 2).astype(jnp.int32)
        self.sign = 1 - 2 * upper
        self.base = upper * (self.planes - 1)
        self.plane = self.base + self.sign * z
        self.corners = {
            "own": corner,
            "beside": y * 2 + (1 - x),
            "across": (1 - y) * 2 + x,
            "opposite": (1 - y) * 2 + (1 - x),
        }
        first = z * CORNERS
        self.target = {
            INNER: (self.row + CORNERS * self.sign, self.col),
            OUTER: (self.row - CORNERS * self.sign, self.col),
            ACROSS_X: (first + self.corners["beside"], self.col),
            ACROSS_Y: (first + self.corners["across"], self.col),
            PARTNER: (self.row, 1 - self.col),
        }

    def source(self, origin, corner):
        return (self.base + self.sign * origin) * CORNERS + self.corners[corner]


def in_plane(planes, plane, origin):
    middle = planes // 2
    if plane < middle:
        return plane <= origin < middle
    return middle <= origin <= plane


def onward(planes, plane, origin, corner, part):
    found = []
    rising = origin <= plane < planes - 1
    falling = origin >= plane > 0
    if corner == "own":
        if rising:
            found.append((INNER, plane + 1, "own"))
        if falling:
            found.append((OUTER, plane - 1, "own"))
        found += [(ACROSS_X, plane, "beside"), (ACROSS_Y, plane, "across")]
    elif corner == "beside":
        if in_plane(planes, plane, origin) and part % 2 == 1:
            found.append((ACROSS_Y, plane, "opposite"))
    elif corner == "across":
        if in_plane(planes, plane, origin) and part % 2 == 0:
            found.append((ACROSS_X, plane, "opposite"))
    else:
        if rising and not in_plane(planes, plane + 1, origin):
            found.append((INNER, plane + 1, "opposite"))
        if falling and not in_plane(planes, plane - 1, origin):
            found.append((OUTER, plane - 1, "opposite"))
    return found


def plan(planes, ready):
    parts = len(ready)
    waiting = {}
    free_at = {}
    acts = [[] for _ in range(planes)]
    events = []
    count = 0
    for plane in range(planes):
        for q in range(parts):
            events.append((ready[q], count, plane, (plane, "own", q), None))
            count += 1
    while events:
        event = min(events)
        events.remove(event)
        now, _, plane, part, link = event
        touched = []
        if link is None:
            origin, corner, q = part
            if (origin, corner) != (plane, "own"):
                acts[plane].append((now, "take", part))
            for out, _, _ in onward(planes, plane, origin, corner, q):
                waiting.setdefault((plane, out), []).append(
                    (abs(plane - origin), now, count, part)
                )
                count += 1
                touched.append((plane, out))
        else:
            touched.append((plane, link))
        for key in touched:
            queue = waiting.get(key, [])
            if not queue or free_at.get(key, -1.0) > now:
                continue
            item = min(queue)
            queue.remove(item)
            free_at[key] = now + SEND_US
            events.append((now + SEND_US, count, plane, None, key[1]))
            count += 1
            sent = item[3]
            if sent[:2] != (plane, "own"):
                acts[plane].append((max(item[1], now - LEAD_US) + 1e-6, "send", key[1], sent))
            for out, to, corner in onward(planes, plane, *sent):
                if out == key[1]:
                    events.append(
                        (now + SEND_US + HOP_US, count, to, (sent[0], corner, sent[2]), None)
                    )
                    count += 1
    return [sorted(found, key=lambda act: act[0]) for found in acts]


class Gather:
    def __init__(self, place, all_ref, parts, recv, passed, met, sent, ready):
        self.place, self.all_ref, self.parts = place, all_ref, parts
        self.recv, self.passed, self.met, self.sent = recv, passed, met, sent
        self.size = all_ref.shape[0] // (place.planes * CORNERS * 2 * parts)
        self.near = range((place.planes + 1) // 2)
        self.acts = plan(place.planes, ready)

    def copy(self, link, part, col=None):
        origin, corner, q = part
        row = self.place.source(origin, corner)
        col = self.place.col if col is None else col
        ref = self.all_ref.at[pl.ds(((row * 2 + col) * self.parts + q) * self.size, self.size)]
        landed = self.recv.at[row, q] if link != PARTNER else self.passed
        return self.describe(ref, link, landed)

    def describe(self, ref, link, landed):
        return pltpu.make_async_remote_copy(
            src_ref=ref,
            dst_ref=ref,
            send_sem=self.sent.at[link],
            recv_sem=landed,
            device_id=self.place.target[link],
            device_id_type=MESH,
        )

    def own(self, q, col=None):
        col = self.place.col if col is None else col
        first = ((self.place.row * 2 + col) * self.parts + q) * self.size
        return self.all_ref.at[pl.ds(first, self.size)]

    def start_own(self, q):
        ref = self.own(q)
        for link in (ACROSS_X, ACROSS_Y, INNER):
            self.describe(ref, link, self.recv.at[self.place.row, q]).start()

        @pl.when(self.place.plane > 0)
        def _():
            self.describe(ref, OUTER, self.recv.at[self.place.row, q]).start()

        self.describe(ref, PARTNER, self.met.at[q]).start()

    def meet(self, q):
        self.describe(self.own(q, 1 - self.place.col), PARTNER, self.met.at[q]).wait_recv()

    def run(self, after, until):
        for plane in self.near:
            chosen = [act for act in self.acts[plane] if after < act[0] <= until]
            if chosen:

                @pl.when(self.place.plane == plane)
                def _(chosen=chosen):
                    for act in chosen:
                        if act[1] == "take":
                            self.copy(INNER, act[2]).wait_recv()
                            self.copy(PARTNER, act[2]).start()
                        else:
                            self.copy(act[2], act[3]).start()

    def all_passed(self):
        count = (self.place.planes * CORNERS - 1) * self.parts * self.size
        self.describe(self.all_ref.at[pl.ds(0, count)], PARTNER, self.passed).wait_recv()

    def all_sent(self):
        for plane in self.near:

            @pl.when(self.place.plane == plane)
            def _(plane=plane):
                counts = [0] * 5
                for act in self.acts[plane]:
                    counts[PARTNER if act[1] == "take" else act[2]] += 1
                for link in range(5):
                    own = self.parts if link != OUTER or plane > 0 else 0
                    total = (counts[link] + own) * self.size
                    if total:
                        ref = self.all_ref.at[pl.ds(0, total)]
                        self.describe(ref, link, self.passed).wait_send()


def greet(place, meanwhile):
    barrier = pltpu.get_barrier_semaphore()
    for link in (ACROSS_X, ACROSS_Y, PARTNER, INNER):
        pl.semaphore_signal(barrier, inc=1, device_id=place.target[link], device_id_type=MESH)

    @pl.when(place.plane > 0)
    def _():
        pl.semaphore_signal(barrier, inc=1, device_id=place.target[OUTER], device_id_type=MESH)

    meanwhile()
    pl.semaphore_wait(barrier, 4 + (place.plane > 0).astype(jnp.int32))


def slot_groups(slot_count):
    return [range(s, min(s + SLOT_GROUP, slot_count)) for s in range(0, slot_count, SLOT_GROUP)]


def mirror_row(a, first_own, pattern, tiles, x_all, y_all, stepped, sample_count):
    slot_count = tiles.shape[1]
    pair_weight = step_size * 0.5 / sample_count
    left = doubled(x_all[first_own + a])
    for group in slot_groups(slot_count):
        found = times_transposed(left, [y_all[pattern[a, s]] for s in group])
        for s, mirror in zip(group, found):
            stepped[a, s] = soft_shrink(
                tiles[a, s] - pair_weight * mirror, step_size * shrink_weight
            )


def sweeps_kernel(
    pattern_in,
    tiles_in,
    diag_in,
    samples,
    tiles,
    x_all,
    y_last,
    diag,
    pattern,
    y_part,
    y_in,
    recv,
    passed,
    met,
    sent,
    local,
    pair,
    *y_before,
):
    place = Place()
    y_every = [*y_before, y_last]
    block_rows, slot_count = tiles.shape[:2]
    diag_blocks = diag_in.shape[0]
    sample_count = x_all.shape[2]
    first_own = place.row * block_rows
    first_diag = place.col * diag_blocks
    first_other = (1 - place.col) * diag_blocks
    load = pltpu.make_async_copy(tiles_in, tiles, local.at[0])
    load_diag = pltpu.make_async_copy(diag_in, diag, local.at[2])
    load_pattern = pltpu.make_async_copy(pattern_in, pattern, local.at[3])
    mine = pl.ds(first_own + first_diag, diag_blocks)
    take = pltpu.make_async_copy(samples, x_all.at[mine], local.at[1])

    def gather(n, all_ref, ready):
        return Gather(
            place, all_ref, diag_blocks, recv.at[n % 2], passed.at[n % 2], met.at[n % 2], sent.at[n % 2], ready
        )

    forever = float("inf")
    gathers = [gather(0, x_all, [0.0] * diag_blocks)]

    def start_loads():
        for copy in (take, load_pattern, load, load_diag):
            copy.start()

    greet(place, start_loads)
    take.wait()
    for q in range(diag_blocks):
        gathers[0].start_own(q)
    gathers[0].run(-1.0, forever)
    for q in range(diag_blocks):
        gathers[0].meet(q)
    gathers[0].all_passed()
    load.wait()
    load_diag.wait()
    load_pattern.wait()

    def y_row(a):
        y_part[a] = product_row(lambda s: tiles[a, s], lambda s: x_all[pattern[a, s]], slot_count)

    def send_partial(sweep, d):
        return pltpu.make_async_remote_copy(
            src_ref=y_part.at[first_other + d],
            dst_ref=y_in.at[sweep, d],
            send_sem=pair.at[0, d],
            recv_sem=pair.at[1, d],
            device_id=place.target[PARTNER],
            device_id_type=MESH,
        )

    groups = slot_groups(slot_count)
    pair_weight = step_size * 0.5 / sample_count

    def cross_tiles(a, y_all):
        left = doubled(y_all[first_own + a])
        for group in groups:
            found = times_transposed(left, [x_all[pattern[a, s]] for s in group])
            for s, cross in zip(group, found):
                tiles[a, s] = (1.0 - step_size * ridge_weight) * tiles[a, s] - pair_weight * cross

    def mirror_tiles(a, y_all):
        mirror_row(a, first_own, pattern, tiles, x_all, y_all, tiles, sample_count)

    def step_own(d, y_all):
        own = first_own + first_diag + d
        pair_sum = (
            times_transposed(doubled(y_all[own]), [x_all[own]])[0]
            + times_transposed(doubled(x_all[own]), [y_all[own]])[0]
        )
        diag[d] = stepped_diag(diag[d], pair_sum, sample_count)

    def products(sweep, before):
        y_all = y_every[sweep]
        row_us = ROW_US[min(sweep, 1)]
        ready = [2 * row_us * d for d in range(diag_blocks)]
        going = gather(1 + sweep, y_all, ready)
        gathers.append(going)

        def finalize(d):
            send_partial(sweep, d).wait()
            y_all[first_own + first_diag + d] = y_part[first_diag + d] + y_in[sweep, d]
            going.start_own(d)

        @pl.loop(0, diag_blocks)
        def _(d):
            before(first_other + d)
            y_row(first_other + d)
            send_partial(sweep, d).start()

            if sweep == 0:

                @pl.when(d > 0)
                def _():
                    finalize(d - 1)

            for k in range(1, diag_blocks):

                @pl.when(d == k)
                def _(k=k):
                    going.run(ready[k - 1] - 2 * row_us, ready[k - 1])

            before(first_diag + d)
            y_row(first_diag + d)
            y_part[first_diag + d] += fold(times(diag[d], x_all[first_own + first_diag + d]))
            if sweep:
                finalize(d)

        if sweep == 0:
            finalize(diag_blocks - 1)

        @pl.loop(0, block_rows)
        def _(n):
            for k in range(block_rows):

                @pl.when(n == k)
                def _(k=k):
                    if k == diag_blocks:
                        for q in range(diag_blocks):
                            going.meet(q)
                    begin = ready[-1] + k * UNIT_US
                    going.run(ready[-2] if k == 0 else begin - UNIT_US, begin)

            cross_tiles((first_diag + n) % block_rows, y_all)

            @pl.when(n < diag_blocks)
            def _():
                step_own(n, y_all)

        gathers[sweep].all_sent()
        going.run(ready[-1] + (block_rows - 1) * UNIT_US, forever)
        going.all_passed()

    products(0, lambda a: None)
    for sweep in range(1, ITERS):
        products(sweep, lambda a: mirror_tiles(a, y_every[sweep - 1]))
    gathers[-1].all_sent()


def finish_kernel(pattern, tiles, x_all, y_all, diag_in, tiles_out, diag_out, ready, sems):
    block_rows, slot_count = tiles.shape[:2]
    sample_count = x_all.shape[2]
    first_own = lax.axis_index("row") * block_rows
    store_diag = pltpu.make_async_copy(diag_in, diag_out, sems.at[block_rows])
    store_diag.start()

    def store(a):
        return pltpu.make_async_copy(ready.at[a], tiles_out.at[a], sems.at[a])

    def rows(first):
        for a in (first, first + 1):
            mirror_row(a, first_own, pattern, tiles, x_all, y_all, ready, sample_count)
            store(a).start()

    pl.loop(0, block_rows, step=2)(rows)

    store_diag.wait()

    @pl.loop(0, block_rows)
    def _(a):
        store(a).wait()


def gathered_sweeps(omega_tiles, omega_diag, samples, pattern):
    block_rows, slot_count, size, _ = omega_tiles.shape
    row_count = lax.axis_size("row")
    sample_count = samples.shape[1]
    diag_blocks = block_rows // lax.axis_size("col")
    diag = omega_diag.reshape(diag_blocks, size, size)
    every = (row_count * block_rows, size, sample_count)
    in_vmem = pl.BlockSpec(memory_space=pltpu.VMEM)
    in_hbm = pl.BlockSpec(memory_space=pltpu.HBM)
    in_smem = pl.BlockSpec(memory_space=pltpu.SMEM)
    tiles, x_all, y_all, diag, listed = pl.pallas_call(
        sweeps_kernel,
        name="sweeps",
        out_shape=[
            pltpu.VMEM(omega_tiles.shape, jnp.float32),
            pltpu.VMEM(every, jnp.float32),
            pltpu.VMEM(every, jnp.float32),
            pltpu.VMEM(diag.shape, jnp.float32),
            pltpu.SMEM(pattern.shape, jnp.int32),
        ],
        in_specs=[in_hbm] * 4,
        out_specs=[in_vmem] * 4 + [in_smem],
        scratch_shapes=[
            pltpu.VMEM((block_rows, size, sample_count), jnp.float32),
            pltpu.VMEM((ITERS, diag_blocks, size, sample_count), jnp.float32),
            pltpu.SemaphoreType.DMA((2, row_count, diag_blocks)),
            pltpu.SemaphoreType.DMA((2,)),
            pltpu.SemaphoreType.DMA((2, diag_blocks)),
            pltpu.SemaphoreType.DMA((2, 5)),
            pltpu.SemaphoreType.DMA((4,)),
            pltpu.SemaphoreType.DMA((2, diag_blocks)),
        ]
        + [pltpu.VMEM(every, jnp.float32)] * (ITERS - 1),
        compiler_params=pltpu.CompilerParams(
            collective_id=0, has_side_effects=True, vmem_limit_bytes=40 * 2**20
        ),
    )(
        *(
            pltpu.with_memory_space_constraint(v, pltpu.HBM)
            for v in (pattern, omega_tiles, diag, samples.reshape(diag_blocks, size, sample_count))
        ),
    )
    held = [pltpu.with_memory_space_constraint(v, pltpu.VMEM) for v in (tiles, x_all, y_all, diag)]
    tiles, diag = pl.pallas_call(
        finish_kernel,
        name="finish",
        out_shape=[
            jax.ShapeDtypeStruct(omega_tiles.shape, jnp.float32),
            jax.ShapeDtypeStruct(diag.shape, jnp.float32),
        ],
        in_specs=[in_smem] + [in_vmem] * 4,
        out_specs=[in_hbm, in_hbm],
        scratch_shapes=[
            pltpu.VMEM(omega_tiles.shape, jnp.float32),
            pltpu.SemaphoreType.DMA((block_rows + 1,)),
        ],
        compiler_params=pltpu.CompilerParams(vmem_limit_bytes=16 * 2**20),
    )(pltpu.with_memory_space_constraint(listed, pltpu.SMEM), *held)
    return tiles, diag.reshape(omega_diag.shape)


def on_device(omega_tiles, omega_diag, samples, pattern):
    row_count = lax.axis_size("row")
    block_rows, slot_count = omega_tiles.shape[:2]
    peer_span = row_count // 2 - 2
    capacity = max(1, (slot_count * block_rows // 2 - 1 + peer_span - 1) // peer_span)
    whole_gather = 2 * capacity >= block_rows and lax.axis_size("col") == 2 and row_count % 8 == 0
    sweeps = gathered_sweeps if whole_gather else listed_sweeps
    return sweeps(omega_tiles, omega_diag, samples, pattern)


def solution(mesh):
    in_specs = (
        P("row", "col", None, None),
        P(("row", "col"), None),
        P(("row", "col"), None),
        P("row", "col"),
    )
    out_specs = (P("row", "col", None, None), P(("row", "col"), None))
    return jax.shard_map(
        on_device, mesh=mesh, in_specs=in_specs, out_specs=out_specs, check_vma=False
    )
```

```python
import jax
import jax.numpy as jnp
from jax import lax
from jax.experimental import pallas as pl
from jax.experimental.pallas import tpu as pltpu
from jax.sharding import PartitionSpec as P

ITERS = 2


step_size = 0.2
shrink_weight = 0.05
ridge_weight = 0.1


def soft_shrink(values, threshold):
    return values - jnp.clip(values, -threshold, threshold)


def listed_sweeps(omega_tiles, omega_diag, samples, pattern):
    highest = lax.Precision.HIGHEST
    row_count = lax.axis_size("row")
    col_count = lax.axis_size("col")
    my_row = lax.axis_index("row")
    my_col = lax.axis_index("col")
    block_rows = omega_tiles.shape[0]
    slot_count = omega_tiles.shape[1]
    block_size = omega_tiles.shape[2]
    sample_count = samples.shape[1]
    diag_blocks = block_rows // col_count
    all_blocks = block_rows * row_count
    peer_span = row_count // 2 - 2
    capacity = max(1, (slot_count * block_rows // 2 - 1 + peer_span - 1) // peer_span)
    tile_count = block_rows * slot_count
    x_rows = lax.all_gather(samples, "col", axis=0, tiled=True)
    x_blocks = x_rows.reshape(block_rows, block_size, sample_count)
    slot_ids = my_col * slot_count + jnp.arange(slot_count, dtype=jnp.int32)
    own_blocks = my_row * block_rows + jnp.arange(block_rows, dtype=jnp.int32)
    peer_row = (pattern // block_rows).reshape(tile_count)
    order_key = (
        slot_ids[None, :] * all_blocks + jnp.minimum(own_blocks[:, None], pattern)
    ).reshape(tile_count)
    same_peer = peer_row[:, None] == peer_row[None, :]
    before = order_key[None, :] < order_key[:, None]
    peer_rank = jnp.sum((same_peer & before).astype(jnp.int32), axis=1)
    dest_slot = peer_row * capacity + peer_rank
    source_row = jnp.arange(tile_count, dtype=jnp.int32) // slot_count

    def pack_slots(values):
        empty_slots = jnp.zeros((row_count * capacity,) + values.shape[1:], jnp.float32)
        return empty_slots.at[dest_slot].set(values)

    def unpack_slots(received):
        return received[dest_slot].reshape((block_rows, slot_count) + received.shape[1:])

    x_tiles = unpack_slots(
        lax.all_to_all(
            pack_slots(x_blocks[source_row]), "row", split_axis=0, concat_axis=0, tiled=True
        )
    )
    first_diag = my_col * diag_blocks
    x_diag = lax.dynamic_slice_in_dim(x_blocks, first_diag, diag_blocks, 0)
    identity = jnp.eye(block_size, dtype=jnp.float32)
    tile_vals = omega_tiles
    diag_vals = omega_diag.reshape(diag_blocks, block_size, block_size)
    for sweep_index in range(ITERS):
        row_terms = jnp.einsum("askm,asmn->akn", tile_vals, x_tiles, precision=highest)
        diag_terms = jnp.einsum("bkm,bmn->bkn", diag_vals, x_diag, precision=highest)
        own_terms = lax.dynamic_slice_in_dim(row_terms, first_diag, diag_blocks, 0) + diag_terms
        row_terms = lax.dynamic_update_slice_in_dim(row_terms, own_terms, first_diag, 0)
        products = lax.psum(row_terms, "col")
        cross_terms = jnp.einsum("akn,asqn->askq", products, x_tiles, precision=highest)
        returned = lax.all_to_all(
            pack_slots(products[source_row]), "row", split_axis=0, concat_axis=0, tiled=True
        )
        mirror = jnp.einsum("akn,asqn->askq", x_blocks, unpack_slots(returned), precision=highest)
        gradient = (cross_terms + mirror) * (0.5 / sample_count) + ridge_weight * tile_vals
        tile_vals = soft_shrink(tile_vals - step_size * gradient, step_size * shrink_weight)
        y_diag = lax.dynamic_slice_in_dim(products, first_diag, diag_blocks, 0)
        self_cross = jnp.einsum("bkn,bqn->bkq", y_diag, x_diag, precision=highest)
        pivots = jnp.diagonal(diag_vals, axis1=1, axis2=2)
        diag_grad = (self_cross + jnp.swapaxes(self_cross, 1, 2)) * (
            0.5 / sample_count
        ) + ridge_weight * diag_vals
        diag_grad = diag_grad - identity * (1.0 / pivots)[:, :, None]
        stepped = diag_vals - step_size * diag_grad
        diag_vals = identity * stepped + (1.0 - identity) * soft_shrink(
            stepped, step_size * shrink_weight
        )
    return (tile_vals, diag_vals.reshape(omega_diag.shape))


def halves(values):
    high = values.astype(jnp.bfloat16)
    low = (values - high.astype(jnp.float32)).astype(jnp.bfloat16)
    return high, low


def stacked(values):
    return jnp.concatenate(halves(values), axis=0)


def beside(values):
    return jnp.concatenate(halves(values), axis=1)


def fold(full):
    rows, cols = full.shape[0] // 2, full.shape[1] // 2
    return full[:rows, :cols] + (full[:rows, cols:] + full[rows:, :cols])


def times(left, right):
    return jnp.dot(stacked(left), beside(right), preferred_element_type=jnp.float32)


def doubled(values):
    tall = stacked(values)
    return jnp.concatenate([tall, tall], axis=1)


def times_transposed(left_doubled, rights):
    right = jnp.concatenate([beside(r) for r in rights], axis=0)
    full = lax.dot_general(
        left_doubled, right, (((1,), (1,)), ((), ())), preferred_element_type=jnp.float32
    )
    rows, cols = full.shape[0] // 2, rights[0].shape[0]
    full = full[:rows] + full[rows:]
    return [full[:, n * cols : (n + 1) * cols] for n in range(len(rights))]


def product_row(tile_of, x_of, slot_count):
    left = jnp.concatenate([tile_of(s) for s in range(slot_count)], axis=1)
    right = jnp.concatenate([x_of(s) for s in range(slot_count)], axis=0)
    return fold(times(left, right))


def stepped_diag(diag, pair_sum, sample_count):
    size = diag.shape[0]
    on_diagonal = lax.broadcasted_iota(jnp.int32, (size, size), 0) == lax.broadcasted_iota(
        jnp.int32, (size, size), 1
    )
    gradient = pair_sum * (0.5 / sample_count) + ridge_weight * diag
    gradient = gradient - jnp.where(on_diagonal, 1.0 / jnp.where(on_diagonal, diag, 1.0), 0.0)
    stepped = diag - step_size * gradient
    return jnp.where(on_diagonal, stepped, soft_shrink(stepped, step_size * shrink_weight))


MESH = pl.DeviceIdType.MESH
CORNERS = 4
SLOT_GROUP = 2
SEND_US = 1.44
HOP_US = 1.7
LEAD_US = 2.5
ROW_US = (0.42, 0.85)
UNIT_US = 1.44
INNER, OUTER, ACROSS_X, ACROSS_Y, PARTNER = range(5)


class Place:
    def __init__(self):
        self.row = lax.axis_index("row")
        self.col = lax.axis_index("col")
        self.planes = lax.axis_size("row") // CORNERS
        z = self.row // CORNERS
        corner = self.row % CORNERS
        y, x = corner // 2, corner % 2
        upper = (z >= self.planes // 2).astype(jnp.int32)
        self.sign = 1 - 2 * upper
        self.base = upper * (self.planes - 1)
        self.plane = self.base + self.sign * z
        self.corners = {
            "own": corner,
            "beside": y * 2 + (1 - x),
            "across": (1 - y) * 2 + x,
            "opposite": (1 - y) * 2 + (1 - x),
        }
        first = z * CORNERS
        self.target = {
            INNER: (self.row + CORNERS * self.sign, self.col),
            OUTER: (self.row - CORNERS * self.sign, self.col),
            ACROSS_X: (first + self.corners["beside"], self.col),
            ACROSS_Y: (first + self.corners["across"], self.col),
            PARTNER: (self.row, 1 - self.col),
        }

    def source(self, origin, corner):
        return (self.base + self.sign * origin) * CORNERS + self.corners[corner]


def in_plane(planes, plane, origin):
    middle = planes // 2
    if plane < middle:
        return plane <= origin < middle
    return middle <= origin <= plane


def onward(planes, plane, origin, corner, part):
    found = []
    rising = origin <= plane < planes - 1
    falling = origin >= plane > 0
    if corner == "own":
        if rising:
            found.append((INNER, plane + 1, "own"))
        if falling:
            found.append((OUTER, plane - 1, "own"))
        found += [(ACROSS_X, plane, "beside"), (ACROSS_Y, plane, "across")]
    elif corner == "beside":
        if in_plane(planes, plane, origin) and part % 2 == 1:
            found.append((ACROSS_Y, plane, "opposite"))
    elif corner == "across":
        if in_plane(planes, plane, origin) and part % 2 == 0:
            found.append((ACROSS_X, plane, "opposite"))
    else:
        if rising and not in_plane(planes, plane + 1, origin):
            found.append((INNER, plane + 1, "opposite"))
        if falling and not in_plane(planes, plane - 1, origin):
            found.append((OUTER, plane - 1, "opposite"))
    return found


def plan(planes, ready):
    parts = len(ready)
    waiting = {}
    free_at = {}
    acts = [[] for _ in range(planes)]
    events = []
    count = 0
    for plane in range(planes):
        for q in range(parts):
            events.append((ready[q], count, plane, (plane, "own", q), None))
            count += 1
    while events:
        event = min(events)
        events.remove(event)
        now, _, plane, part, link = event
        touched = []
        if link is None:
            origin, corner, q = part
            if (origin, corner) != (plane, "own"):
                acts[plane].append((now, "take", part))
            for out, _, _ in onward(planes, plane, origin, corner, q):
                waiting.setdefault((plane, out), []).append(
                    (abs(plane - origin), now, count, part)
                )
                count += 1
                touched.append((plane, out))
        else:
            touched.append((plane, link))
        for key in touched:
            queue = waiting.get(key, [])
            if not queue or free_at.get(key, -1.0) > now:
                continue
            item = min(queue)
            queue.remove(item)
            free_at[key] = now + SEND_US
            events.append((now + SEND_US, count, plane, None, key[1]))
            count += 1
            sent = item[3]
            if sent[:2] != (plane, "own"):
                acts[plane].append((max(item[1], now - LEAD_US) + 1e-6, "send", key[1], sent))
            for out, to, corner in onward(planes, plane, *sent):
                if out == key[1]:
                    events.append(
                        (now + SEND_US + HOP_US, count, to, (sent[0], corner, sent[2]), None)
                    )
                    count += 1
    return [sorted(found, key=lambda act: act[0]) for found in acts]


class Gather:
    def __init__(self, place, all_ref, parts, recv, passed, met, sent, ready):
        self.place, self.all_ref, self.parts = place, all_ref, parts
        self.recv, self.passed, self.met, self.sent = recv, passed, met, sent
        self.size = all_ref.shape[0] // (place.planes * CORNERS * 2 * parts)
        self.near = range((place.planes + 1) // 2)
        self.acts = plan(place.planes, ready)

    def copy(self, link, part, col=None):
        origin, corner, q = part
        row = self.place.source(origin, corner)
        col = self.place.col if col is None else col
        ref = self.all_ref.at[pl.ds(((row * 2 + col) * self.parts + q) * self.size, self.size)]
        landed = self.recv.at[row, q] if link != PARTNER else self.passed
        return self.describe(ref, link, landed)

    def describe(self, ref, link, landed):
        return pltpu.make_async_remote_copy(
            src_ref=ref,
            dst_ref=ref,
            send_sem=self.sent.at[link],
            recv_sem=landed,
            device_id=self.place.target[link],
            device_id_type=MESH,
        )

    def own(self, q, col=None):
        col = self.place.col if col is None else col
        first = ((self.place.row * 2 + col) * self.parts + q) * self.size
        return self.all_ref.at[pl.ds(first, self.size)]

    def start_own(self, q):
        ref = self.own(q)
        for link in (ACROSS_X, ACROSS_Y, INNER):
            self.describe(ref, link, self.recv.at[self.place.row, q]).start()

        @pl.when(self.place.plane > 0)
        def _():
            self.describe(ref, OUTER, self.recv.at[self.place.row, q]).start()

        self.describe(ref, PARTNER, self.met.at[q]).start()

    def meet(self, q):
        self.describe(self.own(q, 1 - self.place.col), PARTNER, self.met.at[q]).wait_recv()

    def run(self, after, until):
        for plane in self.near:
            chosen = [act for act in self.acts[plane] if after < act[0] <= until]
            if chosen:

                @pl.when(self.place.plane == plane)
                def _(chosen=chosen):
                    for act in chosen:
                        if act[1] == "take":
                            self.copy(INNER, act[2]).wait_recv()
                            self.copy(PARTNER, act[2]).start()
                        else:
                            self.copy(act[2], act[3]).start()

    def all_passed(self):
        count = (self.place.planes * CORNERS - 1) * self.parts * self.size
        self.describe(self.all_ref.at[pl.ds(0, count)], PARTNER, self.passed).wait_recv()

    def all_sent(self):
        for plane in self.near:

            @pl.when(self.place.plane == plane)
            def _(plane=plane):
                counts = [0] * 5
                for act in self.acts[plane]:
                    counts[PARTNER if act[1] == "take" else act[2]] += 1
                for link in range(5):
                    own = self.parts if link != OUTER or plane > 0 else 0
                    total = (counts[link] + own) * self.size
                    if total:
                        ref = self.all_ref.at[pl.ds(0, total)]
                        self.describe(ref, link, self.passed).wait_send()


def greet(place, meanwhile):
    barrier = pltpu.get_barrier_semaphore()
    for link in (ACROSS_X, ACROSS_Y, PARTNER, INNER):
        pl.semaphore_signal(barrier, inc=1, device_id=place.target[link], device_id_type=MESH)

    @pl.when(place.plane > 0)
    def _():
        pl.semaphore_signal(barrier, inc=1, device_id=place.target[OUTER], device_id_type=MESH)

    meanwhile()
    pl.semaphore_wait(barrier, 4 + (place.plane > 0).astype(jnp.int32))


def slot_groups(slot_count):
    return [range(s, min(s + SLOT_GROUP, slot_count)) for s in range(0, slot_count, SLOT_GROUP)]


def mirror_row(a, first_own, pattern, tiles, x_all, y_all, stepped, sample_count):
    slot_count = tiles.shape[1]
    pair_weight = step_size * 0.5 / sample_count
    left = doubled(x_all[first_own + a])
    for group in slot_groups(slot_count):
        found = times_transposed(left, [y_all[pattern[a, s]] for s in group])
        for s, mirror in zip(group, found):
            stepped[a, s] = soft_shrink(
                tiles[a, s] - pair_weight * mirror, step_size * shrink_weight
            )


def sweeps_kernel(
    pattern_in,
    tiles_in,
    diag_in,
    samples,
    tiles,
    x_all,
    y_last,
    diag,
    pattern,
    y_part,
    y_in,
    recv,
    passed,
    met,
    sent,
    local,
    pair,
    *y_before,
):
    place = Place()
    y_every = [*y_before, y_last]
    block_rows, slot_count = tiles.shape[:2]
    diag_blocks = diag_in.shape[0]
    sample_count = x_all.shape[2]
    first_own = place.row * block_rows
    first_diag = place.col * diag_blocks
    first_other = (1 - place.col) * diag_blocks
    load = pltpu.make_async_copy(tiles_in, tiles, local.at[0])
    load_diag = pltpu.make_async_copy(diag_in, diag, local.at[2])
    load_pattern = pltpu.make_async_copy(pattern_in, pattern, local.at[3])
    mine = pl.ds(first_own + first_diag, diag_blocks)
    take = pltpu.make_async_copy(samples, x_all.at[mine], local.at[1])

    def gather(n, all_ref, ready):
        return Gather(
            place, all_ref, diag_blocks, recv.at[n % 2], passed.at[n % 2], met.at[n % 2], sent.at[n % 2], ready
        )

    forever = float("inf")
    gathers = [gather(0, x_all, [0.0] * diag_blocks)]

    def start_loads():
        for copy in (take, load_pattern, load, load_diag):
            copy.start()

    greet(place, start_loads)
    take.wait()
    for q in range(diag_blocks):
        gathers[0].start_own(q)
    gathers[0].run(-1.0, forever)
    for q in range(diag_blocks):
        gathers[0].meet(q)
    gathers[0].all_passed()
    load.wait()
    load_diag.wait()
    load_pattern.wait()

    def y_row(a):
        y_part[a] = product_row(lambda s: tiles[a, s], lambda s: x_all[pattern[a, s]], slot_count)

    def send_partial(sweep, d):
        return pltpu.make_async_remote_copy(
            src_ref=y_part.at[first_other + d],
            dst_ref=y_in.at[sweep, d],
            send_sem=pair.at[0, d],
            recv_sem=pair.at[1, d],
            device_id=place.target[PARTNER],
            device_id_type=MESH,
        )

    groups = slot_groups(slot_count)
    pair_weight = step_size * 0.5 / sample_count

    def cross_tiles(a, y_all):
        left = doubled(y_all[first_own + a])
        for group in groups:
            found = times_transposed(left, [x_all[pattern[a, s]] for s in group])
            for s, cross in zip(group, found):
                tiles[a, s] = (1.0 - step_size * ridge_weight) * tiles[a, s] - pair_weight * cross

    def mirror_tiles(a, y_all):
        mirror_row(a, first_own, pattern, tiles, x_all, y_all, tiles, sample_count)

    def step_own(d, y_all):
        own = first_own + first_diag + d
        pair_sum = (
            times_transposed(doubled(y_all[own]), [x_all[own]])[0]
            + times_transposed(doubled(x_all[own]), [y_all[own]])[0]
        )
        diag[d] = stepped_diag(diag[d], pair_sum, sample_count)

    def products(sweep, before):
        y_all = y_every[sweep]
        row_us = ROW_US[min(sweep, 1)]
        ready = [2 * row_us * d for d in range(diag_blocks)]
        going = gather(1 + sweep, y_all, ready)
        gathers.append(going)

        def finalize(d):
            send_partial(sweep, d).wait()
            y_all[first_own + first_diag + d] = y_part[first_diag + d] + y_in[sweep, d]
            going.start_own(d)

        @pl.loop(0, diag_blocks)
        def _(d):
            before(first_other + d)
            y_row(first_other + d)
            send_partial(sweep, d).start()

            if sweep == 0:

                @pl.when(d > 0)
                def _():
                    finalize(d - 1)

            for k in range(1, diag_blocks):

                @pl.when(d == k)
                def _(k=k):
                    going.run(ready[k - 1] - 2 * row_us, ready[k - 1])

            before(first_diag + d)
            y_row(first_diag + d)
            y_part[first_diag + d] += fold(times(diag[d], x_all[first_own + first_diag + d]))
            if sweep:
                finalize(d)

        if sweep == 0:
            finalize(diag_blocks - 1)

        @pl.loop(0, block_rows)
        def _(n):
            for k in range(block_rows):

                @pl.when(n == k)
                def _(k=k):
                    if k == diag_blocks:
                        for q in range(diag_blocks):
                            going.meet(q)
                    begin = ready[-1] + k * UNIT_US
                    going.run(ready[-2] if k == 0 else begin - UNIT_US, begin)

            cross_tiles((first_diag + n) % block_rows, y_all)

            @pl.when(n < diag_blocks)
            def _():
                step_own(n, y_all)

        gathers[sweep].all_sent()
        going.run(ready[-1] + (block_rows - 1) * UNIT_US, forever)
        going.all_passed()

    products(0, lambda a: None)
    for sweep in range(1, ITERS):
        products(sweep, lambda a: mirror_tiles(a, y_every[sweep - 1]))
    gathers[-1].all_sent()


def finish_kernel(pattern, tiles, x_all, y_all, diag_in, tiles_out, diag_out, ready, sems):
    block_rows, slot_count = tiles.shape[:2]
    sample_count = x_all.shape[2]
    first_own = lax.axis_index("row") * block_rows
    store_diag = pltpu.make_async_copy(diag_in, diag_out, sems.at[block_rows])
    store_diag.start()

    def store(a):
        return pltpu.make_async_copy(ready.at[a], tiles_out.at[a], sems.at[a])

    def rows(first, count):
        for a in range(first, first + count):
            mirror_row(a, first_own, pattern, tiles, x_all, y_all, ready, sample_count)
            store(a).start()

    rows(0, block_rows // 2)
    rows(block_rows // 2, block_rows // 4)
    rows(block_rows // 2 + block_rows // 4, block_rows - block_rows // 2 - block_rows // 4)

    store_diag.wait()

    @pl.loop(0, block_rows)
    def _(a):
        store(a).wait()


def gathered_sweeps(omega_tiles, omega_diag, samples, pattern):
    block_rows, slot_count, size, _ = omega_tiles.shape
    row_count = lax.axis_size("row")
    sample_count = samples.shape[1]
    diag_blocks = block_rows // lax.axis_size("col")
    diag = omega_diag.reshape(diag_blocks, size, size)
    every = (row_count * block_rows, size, sample_count)
    in_vmem = pl.BlockSpec(memory_space=pltpu.VMEM)
    in_hbm = pl.BlockSpec(memory_space=pltpu.HBM)
    in_smem = pl.BlockSpec(memory_space=pltpu.SMEM)
    tiles, x_all, y_all, diag, listed = pl.pallas_call(
        sweeps_kernel,
        name="sweeps",
        out_shape=[
            pltpu.VMEM(omega_tiles.shape, jnp.float32),
            pltpu.VMEM(every, jnp.float32),
            pltpu.VMEM(every, jnp.float32),
            pltpu.VMEM(diag.shape, jnp.float32),
            pltpu.SMEM(pattern.shape, jnp.int32),
        ],
        in_specs=[in_hbm] * 4,
        out_specs=[in_vmem] * 4 + [in_smem],
        scratch_shapes=[
            pltpu.VMEM((block_rows, size, sample_count), jnp.float32),
            pltpu.VMEM((ITERS, diag_blocks, size, sample_count), jnp.float32),
            pltpu.SemaphoreType.DMA((2, row_count, diag_blocks)),
            pltpu.SemaphoreType.DMA((2,)),
            pltpu.SemaphoreType.DMA((2, diag_blocks)),
            pltpu.SemaphoreType.DMA((2, 5)),
            pltpu.SemaphoreType.DMA((4,)),
            pltpu.SemaphoreType.DMA((2, diag_blocks)),
        ]
        + [pltpu.VMEM(every, jnp.float32)] * (ITERS - 1),
        compiler_params=pltpu.CompilerParams(
            collective_id=0, has_side_effects=True, vmem_limit_bytes=40 * 2**20
        ),
    )(
        *(
            pltpu.with_memory_space_constraint(v, pltpu.HBM)
            for v in (pattern, omega_tiles, diag, samples.reshape(diag_blocks, size, sample_count))
        ),
    )
    held = [pltpu.with_memory_space_constraint(v, pltpu.VMEM) for v in (tiles, x_all, y_all, diag)]
    tiles, diag = pl.pallas_call(
        finish_kernel,
        name="finish",
        out_shape=[
            jax.ShapeDtypeStruct(omega_tiles.shape, jnp.float32),
            jax.ShapeDtypeStruct(diag.shape, jnp.float32),
        ],
        in_specs=[in_smem] + [in_vmem] * 4,
        out_specs=[in_hbm, in_hbm],
        scratch_shapes=[
            pltpu.VMEM(omega_tiles.shape, jnp.float32),
            pltpu.SemaphoreType.DMA((block_rows + 1,)),
        ],
        compiler_params=pltpu.CompilerParams(vmem_limit_bytes=16 * 2**20),
    )(pltpu.with_memory_space_constraint(listed, pltpu.SMEM), *held)
    return tiles, diag.reshape(omega_diag.shape)


def on_device(omega_tiles, omega_diag, samples, pattern):
    row_count = lax.axis_size("row")
    block_rows, slot_count = omega_tiles.shape[:2]
    peer_span = row_count // 2 - 2
    capacity = max(1, (slot_count * block_rows // 2 - 1 + peer_span - 1) // peer_span)
    whole_gather = 2 * capacity >= block_rows and lax.axis_size("col") == 2 and row_count % 8 == 0
    sweeps = gathered_sweeps if whole_gather else listed_sweeps
    return sweeps(omega_tiles, omega_diag, samples, pattern)


def solution(mesh):
    in_specs = (
        P("row", "col", None, None),
        P(("row", "col"), None),
        P(("row", "col"), None),
        P("row", "col"),
    )
    out_specs = (P("row", "col", None, None), P(("row", "col"), None))
    return jax.shard_map(
        on_device, mesh=mesh, in_specs=in_specs, out_specs=out_specs, check_vma=False
    )
```
